256 devices in a mesh: dp: 32 (over x, z), ctx: 8 (over y, core).
Axes of the slice: x: 4, y: 4, z: 8, core: 2. Of those that a mesh axis runs over, the one named last changes fastest.
Arguments:
- layer_input: bfloat16 [32, 1024, 4096], P('dp', 'ctx'), may hold values from -6 to 6
- queries: bfloat16 [32, 1024, 4096], P('dp', 'ctx'), may hold values from -4.5 to 4.5
- keys_saved: bfloat16 [32, 1024, 1024], P('dp', 'ctx'), may hold values from -4.5 to 4.5
- values_saved: bfloat16 [32, 1024, 1024], P('dp', 'ctx'), may hold values from -6 to 6
- out_grad: bfloat16 [32, 1024, 4096], P('dp', 'ctx'), may hold values from -6 to 6
- master_weight: float32 [4096, 6144], P('dp', 'ctx'), may hold values from -2 to 2
- first_moment: float32 [4096, 6144], P('dp', 'ctx'), may hold values from -100 to 100
- second_moment: float32 [4096, 6144], P('dp', 'ctx'), may hold values from 10 to 3000
Outputs:
- first_new: float32 [4096, 6144], P('dp', 'ctx')
- second_new: float32 [4096, 6144], P('dp', 'ctx')
- lamb_update: float32 [4096, 6144], P('dp', 'ctx')
- new_weights: bfloat16 [4096, 6144], P(None, 'ctx')
The draws below stay inside these ranges and needn't reach their ends.
All inputs are finite; a program needn't handle non-finite values.
Results may differ from the reference program's by a relative error of at most 0.0095.
Values may be sent and summed in bfloat16 or wider, within the bound.
No kernel may reach another device: no remote copies, remote signals or barrier semaphores. Data moves between devices by JAX's collectives and lax.ppermute only.
A program may use at most 128 MiB of HBM per device.

```python
import math
import jax
import jax.numpy as jnp
from jax import lax

D = 4096
HEADS = 32
KV_HEADS = 8
HEAD_DIM = 128
STEP = 100
BATCH = 32
SEQ_LEN = 1024
GROUP = 4
QKV_COLS = 6144


def draw_queries(key, part):
    shape = (BATCH, SEQ_LEN, HEADS * HEAD_DIM)
    values = jnp.clip(jax.random.normal(jax.random.fold_in(key, 12), shape, jnp.float32), -4.0, 4.0)
    return values.astype(jnp.bfloat16)


def draw_keys_saved(key, part):
    shape = (BATCH, SEQ_LEN, KV_HEADS * HEAD_DIM)
    values = jnp.clip(jax.random.normal(jax.random.fold_in(key, 22), shape, jnp.float32), -4.0, 4.0)
    return values.astype(jnp.bfloat16)


def scaled_matrix(key, divisor, limit):
    row_scale = 10.0 ** (jnp.arange(D, dtype=jnp.float32) / D)
    base = jnp.clip(jax.random.normal(jax.random.fold_in(key, 32), (D, QKV_COLS), jnp.float32), -4.0, 4.0)
    col_scale = 10.0 ** jax.random.uniform(jax.random.fold_in(key, 33), (QKV_COLS,), jnp.float32)
    return jnp.clip(base * row_scale[:, None] * col_scale[None, :] / divisor, -limit, limit)


def draw_master_weight(key, part):
    return scaled_matrix(jax.random.fold_in(key, 41), 3.0 * D ** 0.5, 2.0)


def draw_first_moment(key, part):
    return scaled_matrix(jax.random.fold_in(key, 42), 1.0, 100.0)


def spiked(values, stream_key, source, target, shards_of, factor):
    owner, partner = [(jnp.arange(values.shape[position]) // (values.shape[position] // shards_of)).reshape([-1 if axis == position else 1 for axis in range(values.ndim)]) for position in (source, target)]
    chosen = jax.random.permutation(stream_key, shards_of)[partner]
    strong = (owner == chosen) | (owner == (partner + shards_of // 2) % shards_of)
    return jnp.where(strong, factor * values, values)


def levels(own_key, dims, shards, low, top_value):
    level = 1.0
    for dim, shards_of in shards:
        heights = jax.random.uniform(jax.random.fold_in(jax.random.fold_in(own_key, 6), dim), (shards_of,), jnp.float32, low / len(shards), top_value / len(shards))
        level = level * jnp.repeat(jnp.exp(heights), dims[dim] // shards_of).reshape((-1,) + (1,) * (len(dims) - 1 - dim))
    return level


def scatter_about(own_key, extent, width, most, pieces=(), kind=jnp.bfloat16):
    drawn = jax.random.normal(own_key, extent, jnp.float32) * width
    if len(pieces) > 0:
        drawn = levels(own_key, extent, pieces, -0.22, 0.18) * drawn
    return jnp.clip(drawn, min=-most, max=most).astype(kind)


def heavy_noise(rng, dims, deviation, most, split, heavy, kind=jnp.bfloat16):
    drawn = deviation * jax.random.normal(rng, dims, jnp.float32)
    if split:
        drawn = drawn * levels(rng, dims, split, -0.22, 0.18)
    return jnp.clip(spiked(drawn, jax.random.fold_in(rng, 3), *heavy), -most, most).astype(kind)


def setup_inputs(seed: int = 0) -> dict:
    streams_of = jax.random.split(jax.random.key(seed), 9)
    return {
        "layer_input": heavy_noise(streams_of[0], (BATCH, SEQ_LEN, D), 1.0, 6.0, ((0, 32), (1, 8)), (0, 2, 32, 2.75)),
        "queries": draw_queries(jax.random.fold_in(streams_of[8], 71), 0),
        "keys_saved": draw_keys_saved(jax.random.fold_in(streams_of[8], 71), 0),
        "values_saved": scatter_about(streams_of[3], (BATCH, SEQ_LEN, KV_HEADS * HEAD_DIM), 1.0, 6.0, ((0, 32), (1, 8))),
        "out_grad": scatter_about(streams_of[4], (BATCH, SEQ_LEN, HEADS * HEAD_DIM), 1.0, 6.0, ((0, 32), (1, 8))),
        "master_weight": draw_master_weight(jax.random.fold_in(streams_of[8], 71), 0),
        "first_moment": draw_first_moment(jax.random.fold_in(streams_of[8], 71), 0),
        "second_moment": jnp.clip(jnp.exp(math.log(3000.0) - 5.7037825 * jax.random.uniform(streams_of[7], (D, QKV_COLS), jnp.float32) ** levels(streams_of[7], (D, QKV_COLS), ((0, 32), (1, 8)), -0.2, 0.2)), 10.0, 3000.0),
    }


beta_first = 0.9
beta_second = 0.999
adam_epsilon = 1e-06
decay_rate = 0.01
learn_rate = 0.01
masked_score = -1e+30

def sequence_grads(query_seq, key_seq, value_seq, grad_seq):
    length = query_seq.shape[0]
    score_scale = HEAD_DIM ** (-0.5)
    query_f = query_seq.astype(jnp.float32).reshape(length, KV_HEADS, GROUP, HEAD_DIM)
    key_f = key_seq.astype(jnp.float32).reshape(length, KV_HEADS, HEAD_DIM)
    value_f = value_seq.astype(jnp.float32).reshape(length, KV_HEADS, HEAD_DIM)
    grad_f = grad_seq.astype(jnp.float32).reshape(length, KV_HEADS, GROUP, HEAD_DIM)
    scores = jnp.einsum('qgrd,kgd->grqk', query_f, key_f) * score_scale
    positions = jnp.arange(length)
    allowed = positions[None, :] <= positions[:, None]
    scores = jnp.where(allowed, scores, masked_score)
    probabilities = jax.nn.softmax(scores, axis=-1)
    probs_b = probabilities.astype(jnp.bfloat16).astype(jnp.float32)
    attended = jnp.einsum('grqk,kgd->qgrd', probs_b, value_f)
    row_delta = lax.optimization_barrier(jnp.sum(grad_f * attended, axis=-1))
    prob_grad = jnp.einsum('qgrd,kgd->grqk', grad_f, value_f)
    dscore = probabilities * (prob_grad - jnp.transpose(row_delta, (1, 2, 0))[..., None])
    dscore_b = dscore.astype(jnp.bfloat16).astype(jnp.float32)
    query_grad = (jnp.einsum('grqk,kgd->qgrd', dscore_b, key_f) * score_scale).astype(jnp.bfloat16)
    key_grad = (jnp.einsum('grqk,qgrd->kgd', dscore_b, query_f) * score_scale).astype(jnp.bfloat16)
    value_grad = jnp.einsum('grqk,qgrd->kgd', probs_b, grad_f).astype(jnp.bfloat16)
    joined = jnp.concatenate([query_grad.reshape(length, KV_HEADS, GROUP * HEAD_DIM), key_grad, value_grad], axis=2)
    return joined.reshape(length, QKV_COLS)

def reference(layer_input, queries, keys_saved, values_saved, out_grad, master_weight, first_moment, second_moment):

    def per_sequence(running, seq_items):
        input_seq, query_seq, key_seq, value_seq, grad_seq = seq_items
        grouped = sequence_grads(query_seq, key_seq, value_seq, grad_seq)
        partial_value = jnp.dot(input_seq.T, grouped, preferred_element_type=jnp.float32).astype(jnp.bfloat16)
        return (running + partial_value.astype(jnp.float32), None)
    gradient, unused = lax.scan(per_sequence, jnp.zeros((D, QKV_COLS), jnp.float32), (layer_input, queries, keys_saved, values_saved, out_grad))
    first_new = beta_first * first_moment + (1.0 - beta_first) * gradient
    second_new = beta_second * second_moment + (1.0 - beta_second) * gradient * gradient
    corr_first = 1.0 - beta_first ** STEP
    corr_second = 1.0 - beta_second ** STEP
    direction = first_new / corr_first / (jnp.sqrt(second_new / corr_second) + adam_epsilon) + decay_rate * master_weight
    trust_ratio = jnp.sqrt(jnp.sum(master_weight * master_weight)) / jnp.sqrt(jnp.sum(direction * direction))
    lamb_update = trust_ratio * direction
    new_weights = (master_weight - learn_rate * lamb_update).astype(jnp.bfloat16)
    return (first_new, second_new, lamb_update, new_weights)
```

```python
import jax
import jax.numpy as jnp
from jax import lax
from jax.experimental import pallas as pl
from jax.experimental.pallas import tpu as pltpu
from jax.sharding import Mesh
from jax.sharding import PartitionSpec as P

HEAD_DIM = 128
STEP = 100
GROUP = 4
NX, NZ, NY, NCORE = 4, 8, 4, 2
LENGTH = 1024
COLS = 768
WIDTH = 4096
ROWS = 128
PACKED = 1280
BLOCK = 256

beta_first = 0.9
beta_second = 0.999
adam_epsilon = 1e-06
decay_rate = 0.01
learn_rate = 0.01
masked_score = -1e30
score_scale = HEAD_DIM ** (-0.5)
LOG2E = 1.4426950408889634

f32 = jnp.float32
bf16 = jnp.bfloat16


def dot(a, b, ca, cb):
    return lax.dot_general(a, b, (((ca,), (cb,)), ((), ())), preferred_element_type=f32)


def pack_kernel(q_ref, k_ref, v_ref, g_ref, out_ref):
    out_ref[0, :, 0:512] = q_ref[...]
    out_ref[0, :, 512:640] = k_ref[...]
    out_ref[0, :, 640:768] = v_ref[...]
    out_ref[0, :, 768:1280] = g_ref[...]


def pack(q, k, v, g):
    rows = q.shape[0]
    return pl.pallas_call(
        pack_kernel,
        grid=(8,),
        in_specs=[
            pl.BlockSpec((rows, 512), lambda c: (0, c)),
            pl.BlockSpec((rows, 128), lambda c: (0, c)),
            pl.BlockSpec((rows, 128), lambda c: (0, c)),
            pl.BlockSpec((rows, 512), lambda c: (0, c)),
        ],
        out_specs=pl.BlockSpec((1, rows, PACKED), lambda c: (c, 0, 0)),
        out_shape=jax.ShapeDtypeStruct((8, rows, PACKED), bf16),
        cost_estimate=pl.CostEstimate(flops=0, bytes_accessed=5 << 20, transcendentals=0),
        name="pack",
    )(q, k, v, g)


def attention_kernel(q_ref, k_ref, v_ref, g_ref, dq_ref, dkv_ref, kt_ref, dk_acc, dv_acc):
    head = pl.program_id(0)

    @pl.when(head == 0)
    def _():
        kt_ref[...] = k_ref[...].T
        dk_acc[...] = jnp.zeros_like(dk_acc)
        dv_acc[...] = jnp.zeros_like(dv_acc)

    key_pos = lax.broadcasted_iota(jnp.int32, (BLOCK, BLOCK), 0)
    query_pos = lax.broadcasted_iota(jnp.int32, (BLOCK, BLOCK), 1)
    allowed = key_pos <= query_pos
    for i in range(LENGTH // BLOCK):
        lo, hi = i * BLOCK, (i + 1) * BLOCK
        q = q_ref[lo:hi, :]
        g = g_ref[lo:hi, :]
        scores = dot(k_ref[:hi, :], q, 1, 1)
        diag = jnp.where(allowed, scores[lo:hi, :], masked_score)
        scores = diag if i == 0 else jnp.concatenate([scores[:lo, :], diag], axis=0)
        top = jnp.max(scores, axis=0, keepdims=True)
        weights = jnp.exp2((scores - top) * (score_scale * LOG2E))
        probs = weights * (1.0 / jnp.sum(weights, axis=0, keepdims=True))
        probs_b = probs.astype(bf16)
        prob_grad = dot(v_ref[:hi, :], g, 1, 1)
        row_delta = jnp.sum(probs_b.astype(f32) * prob_grad, axis=0, keepdims=True)
        dscore = (probs * (prob_grad - row_delta)).astype(bf16)
        dq_t = dot(kt_ref[:, :hi], dscore, 1, 0) * score_scale
        dq_ref[:, lo:hi] = dq_t.astype(bf16)
        dk_acc[:hi, :] += dot(dscore, q, 1, 0)
        dv_acc[:hi, :] += dot(probs_b, g, 1, 0)

    @pl.when(head == GROUP - 1)
    def _():
        dkv_ref[0:128, :] = (dk_acc[...] * score_scale).astype(bf16).T
        dkv_ref[128:256, :] = dv_acc[...].astype(bf16).T


def attention(packed):
    return pl.pallas_call(
        attention_kernel,
        grid=(GROUP,),
        in_specs=[
            pl.BlockSpec((LENGTH, 128), lambda h: (0, h)),
            pl.BlockSpec((LENGTH, 128), lambda h: (0, 4)),
            pl.BlockSpec((LENGTH, 128), lambda h: (0, 5)),
            pl.BlockSpec((LENGTH, 128), lambda h: (0, 6 + h)),
        ],
        out_specs=[
            pl.BlockSpec((128, LENGTH), lambda h: (h, 0)),
            pl.BlockSpec((256, LENGTH), lambda h: (0, 0)),
        ],
        out_shape=[
            jax.ShapeDtypeStruct((512, LENGTH), bf16),
            jax.ShapeDtypeStruct((256, LENGTH), bf16),
        ],
        scratch_shapes=[
            pltpu.VMEM((128, LENGTH), bf16),
            pltpu.VMEM((LENGTH, 128), f32),
            pltpu.VMEM((LENGTH, 128), f32),
        ],
        compiler_params=pltpu.CompilerParams(vmem_limit_bytes=48 << 20),
        cost_estimate=pl.CostEstimate(
            flops=4 << 30, bytes_accessed=5 << 20, transcendentals=4 << 20
        ),
        name="attention_backward",
    )(packed, packed, packed, packed)


def project_kernel(dq_ref, dkv_ref, x0, x1, x2, x3, out_ref):
    for i, x_ref in enumerate((x0, x1, x2, x3)):
        out_ref[0, i, 0:512, :] = dot(dq_ref[...], x_ref[...], 1, 0).astype(bf16)
        out_ref[0, i, 512:768, :] = dot(dkv_ref[...], x_ref[...], 1, 0).astype(bf16)


def project(dq, dkv, x):
    def x_spec(i):
        return pl.BlockSpec((LENGTH, ROWS), lambda z: (0, i * NZ + z))

    return pl.pallas_call(
        project_kernel,
        grid=(NZ,),
        in_specs=[
            pl.BlockSpec((512, LENGTH), lambda z: (0, 0)),
            pl.BlockSpec((256, LENGTH), lambda z: (0, 0)),
            *[x_spec(i) for i in range(NX)],
        ],
        out_specs=pl.BlockSpec((1, NX, COLS, ROWS), lambda z: (z, 0, 0, 0)),
        out_shape=jax.ShapeDtypeStruct((NZ, NX, COLS, ROWS), bf16),
        compiler_params=pltpu.CompilerParams(vmem_limit_bytes=48 << 20),
        cost_estimate=pl.CostEstimate(flops=6 << 30, bytes_accessed=16 << 20, transcendentals=0),
        name="project",
    )(dq, dkv, x, x, x, x)


def optimizer_kernel(grad_ref, w_ref, m_ref, v_ref, m_out, v_out, dir_out, sums_out):
    gradient = grad_ref[...].astype(f32).T
    weight = w_ref[...]
    first_new = beta_first * m_ref[...] + (1.0 - beta_first) * gradient
    second_new = beta_second * v_ref[...] + (1.0 - beta_second) * gradient * gradient
    corr_first = 1.0 - beta_first**STEP
    corr_second = 1.0 - beta_second**STEP
    direction = (
        first_new / corr_first / (jnp.sqrt(second_new / corr_second) + adam_epsilon)
        + decay_rate * weight
    )
    m_out[...] = first_new
    v_out[...] = second_new
    dir_out[...] = direction
    weight_sq = jnp.sum(weight * weight)
    update_sq = jnp.sum(direction * direction)
    row = lax.broadcasted_iota(jnp.int32, (8, 128), 0)
    sums_out[...] = jnp.where(row == 0, weight_sq, update_sq)


def optimizer(grad, w, m, v):
    shape = jax.ShapeDtypeStruct((ROWS, COLS), f32)
    return pl.pallas_call(
        optimizer_kernel,
        out_shape=[shape, shape, shape, jax.ShapeDtypeStruct((8, 128), f32)],
        compiler_params=pltpu.CompilerParams(vmem_limit_bytes=32 << 20),
        name="optimizer",
    )(grad, w, m, v)


def all_sum(sums, axes, size):
    spread = jnp.broadcast_to(sums[None], (size,) + sums.shape)
    return jnp.sum(lax.all_to_all(spread, axes, 0, 0, tiled=True), axis=0)


def body(x, q, k, v, g, w, m, s):
    packed = pack(q[0], k[0], v[0], g[0])
    heads = lax.all_to_all(packed, ("y", "core"), 0, 0, tiled=True).reshape(LENGTH, PACKED)
    x_full = lax.all_gather(x[0], ("y", "core"), axis=0, tiled=True)
    dq, dkv = attention(heads)
    partial = project(dq, dkv, x_full)
    partial = lax.psum_scatter(partial, "z", scatter_dimension=0, tiled=True)[0]
    grad = lax.psum_scatter(partial, "x", scatter_dimension=0, tiled=True)[0]
    first_new, second_new, direction, sums = optimizer(grad, w, m, s)
    sums = all_sum(all_sum(sums, ("y", "core"), 8), ("x", "z"), 32)
    trust_ratio = jnp.sqrt(sums[0, 0]) / jnp.sqrt(sums[1, 0])
    lamb_update = trust_ratio * direction
    new_local = (w - learn_rate * lamb_update).astype(bf16)
    new_weights = lax.all_gather(new_local, ("x", "z"), axis=0, tiled=True)
    return first_new, second_new, lamb_update, new_weights


def solution(mesh):
    fine = Mesh(mesh.devices.reshape(NX, NZ, NY, NCORE), ("x", "z", "y", "core"))
    dp, ctx = ("x", "z"), ("y", "core")
    seq = P(dp, ctx, None)
    mat = P(dp, ctx)
    return jax.shard_map(
        body,
        mesh=fine,
        in_specs=(seq, seq, seq, seq, seq, mat, mat, mat),
        out_specs=(mat, mat, mat, P(None, ctx)),
        check_vma=False,
    )
```

```python
import jax
import jax.numpy as jnp
from jax import lax
from jax.experimental import pallas as pl
from jax.experimental.pallas import tpu as pltpu
from jax.sharding import Mesh
from jax.sharding import PartitionSpec as P

HEAD_DIM = 128
STEP = 100
GROUP = 4
NX, NZ, NY, NCORE = 4, 8, 4, 2
LENGTH = 1024
COLS = 768
WIDTH = 4096
ROWS = 128
PACKED = 1280
BLOCK = 256
COLS_A = 448
COLS_B = COLS - COLS_A
ROWS_A = 64
ROWS_B = ROWS - ROWS_A

beta_first = 0.9
beta_second = 0.999
adam_epsilon = 1e-06
decay_rate = 0.01
learn_rate = 0.01
masked_score = -1e30
score_scale = HEAD_DIM ** (-0.5)
LOG2E = 1.4426950408889634

f32 = jnp.float32
bf16 = jnp.bfloat16


def dot(a, b, ca, cb):
    return lax.dot_general(a, b, (((ca,), (cb,)), ((), ())), preferred_element_type=f32)


def pack_kernel(q_ref, k_ref, v_ref, g_ref, out_ref):
    for c in range(out_ref.shape[0]):
        out_ref[c, :, 0:512] = q_ref[:, c * 512 : (c + 1) * 512]
        out_ref[c, :, 512:640] = k_ref[:, c * 128 : (c + 1) * 128]
        out_ref[c, :, 640:768] = v_ref[:, c * 128 : (c + 1) * 128]
        out_ref[c, :, 768:1280] = g_ref[:, c * 512 : (c + 1) * 512]


def pack(q, k, v, g):
    rows = q.shape[0]
    each = 4
    return pl.pallas_call(
        pack_kernel,
        grid=(8 // each,),
        in_specs=[
            pl.BlockSpec((rows, 512 * each), lambda c: (0, c)),
            pl.BlockSpec((rows, 128 * each), lambda c: (0, c)),
            pl.BlockSpec((rows, 128 * each), lambda c: (0, c)),
            pl.BlockSpec((rows, 512 * each), lambda c: (0, c)),
        ],
        out_specs=pl.BlockSpec((each, rows, PACKED), lambda c: (c, 0, 0)),
        out_shape=jax.ShapeDtypeStruct((8, rows, PACKED), bf16),
        cost_estimate=pl.CostEstimate(flops=0, bytes_accessed=5 << 20, transcendentals=0),
        name="pack",
    )(q, k, v, g)


def attention_kernel(q_ref, k_ref, v_ref, g_ref, out_ref, kt_ref, dk_acc, dv_acc):
    head = pl.program_id(0)

    @pl.when(head == 0)
    def _():
        kt_ref[...] = k_ref[...].T
        dk_acc[...] = jnp.zeros_like(dk_acc)
        dv_acc[...] = jnp.zeros_like(dv_acc)

    key_pos = lax.broadcasted_iota(jnp.int32, (BLOCK, BLOCK), 0)
    query_pos = lax.broadcasted_iota(jnp.int32, (BLOCK, BLOCK), 1)
    allowed = key_pos <= query_pos
    for i in range(LENGTH // BLOCK):
        lo, hi = i * BLOCK, (i + 1) * BLOCK
        q = q_ref[lo:hi, :]
        g = g_ref[lo:hi, :]
        scores = dot(k_ref[:hi, :], q, 1, 1)
        diag = jnp.where(allowed, scores[lo:hi, :], masked_score)
        scores = diag if i == 0 else jnp.concatenate([scores[:lo, :], diag], axis=0)
        top = jnp.max(scores, axis=0, keepdims=True)
        weights = jnp.exp2((scores - top) * (score_scale * LOG2E))
        probs = weights * (1.0 / jnp.sum(weights, axis=0, keepdims=True))
        probs_b = probs.astype(bf16)
        prob_grad = dot(v_ref[:hi, :], g, 1, 1)
        row_delta = jnp.sum(probs_b.astype(f32) * prob_grad, axis=0, keepdims=True)
        dscore = (probs * (prob_grad - row_delta)).astype(bf16)
        dq_t = dot(kt_ref[:, :hi], dscore, 1, 0) * score_scale
        out_ref[pl.ds(pl.multiple_of(head * 128, 128), 128), lo:hi] = dq_t.astype(bf16)
        dk_acc[:hi, :] += dot(dscore, q, 1, 0)
        dv_acc[:hi, :] += dot(probs_b, g, 1, 0)

    @pl.when(head == GROUP - 1)
    def _():
        out_ref[512:640, :] = (dk_acc[...] * score_scale).astype(bf16).T
        out_ref[640:768, :] = dv_acc[...].astype(bf16).T


def attention(packed):
    return pl.pallas_call(
        attention_kernel,
        grid=(GROUP,),
        in_specs=[
            pl.BlockSpec((LENGTH, 128), lambda h: (0, h)),
            pl.BlockSpec((LENGTH, 128), lambda h: (0, 4)),
            pl.BlockSpec((LENGTH, 128), lambda h: (0, 5)),
            pl.BlockSpec((LENGTH, 128), lambda h: (0, 6 + h)),
        ],
        out_specs=pl.BlockSpec((COLS, LENGTH), lambda h: (0, 0)),
        out_shape=jax.ShapeDtypeStruct((COLS, LENGTH), bf16),
        scratch_shapes=[
            pltpu.VMEM((128, LENGTH), bf16),
            pltpu.VMEM((LENGTH, 128), f32),
            pltpu.VMEM((LENGTH, 128), f32),
        ],
        compiler_params=pltpu.CompilerParams(vmem_limit_bytes=48 << 20),
        cost_estimate=pl.CostEstimate(
            flops=4 << 30, bytes_accessed=5 << 20, transcendentals=4 << 20
        ),
        name="attention_backward",
    )(packed, packed, packed, packed)


def project(grouped, x, lo, hi, z_major):
    cols = hi - lo
    tile = 4

    def kernel(grouped_ref, x_ref, out_ref):
        res = dot(grouped_ref[lo:hi, :], x_ref[...], 1, 0).astype(bf16)
        for i in range(tile):
            piece = res[:, i * ROWS : (i + 1) * ROWS]
            if z_major:
                out_ref[i, 0] = piece
            else:
                out_ref[0, i] = piece

    if z_major:
        shape, block = (NZ, NX, cols, ROWS), (tile, 1, cols, ROWS)
        place = lambda x, z: (z, x, 0, 0)
    else:
        shape, block = (NX, NZ, cols, ROWS), (1, tile, cols, ROWS)
        place = lambda x, z: (x, z, 0, 0)
    return pl.pallas_call(
        kernel,
        grid=(NX, NZ // tile),
        in_specs=[
            pl.BlockSpec((COLS, LENGTH), lambda x, z: (0, 0)),
            pl.BlockSpec((LENGTH, ROWS * tile), lambda x, z: (0, x * (NZ // tile) + z)),
        ],
        out_specs=pl.BlockSpec(block, place),
        out_shape=jax.ShapeDtypeStruct(shape, bf16),
        compiler_params=pltpu.CompilerParams(vmem_limit_bytes=48 << 20),
        cost_estimate=pl.CostEstimate(
            flops=2 * cols * LENGTH * WIDTH,
            bytes_accessed=(10 << 20) + 2 * cols * WIDTH,
            transcendentals=0,
        ),
        name="project_z" if z_major else "project_x",
    )(grouped, x)


def optimizer_kernel(ga_ref, gb_ref, w_ref, m_ref, v_ref, m_out, v_out, dir_out, a_out, b_out, sums_out):
    grad_a = jnp.sum(ga_ref[...].astype(f32), axis=0)
    grad_b = jnp.sum(gb_ref[...].astype(f32), axis=0)
    gradient = jnp.concatenate([grad_a, grad_b], axis=0).T
    weight = w_ref[...]
    first_new = beta_first * m_ref[...] + (1.0 - beta_first) * gradient
    second_new = beta_second * v_ref[...] + (1.0 - beta_second) * gradient * gradient
    corr_first = 1.0 - beta_first**STEP
    corr_second = 1.0 - beta_second**STEP
    direction = (
        first_new / corr_first / (jnp.sqrt(second_new / corr_second) + adam_epsilon)
        + decay_rate * weight
    )
    m_out[...] = first_new
    v_out[...] = second_new
    dir_out[...] = direction
    a_out[0] = direction[:ROWS_A].astype(bf16)
    a_out[1] = weight[:ROWS_A].astype(bf16)
    b_out[0] = direction[ROWS_A:].astype(bf16)
    b_out[1] = weight[ROWS_A:].astype(bf16)
    weight_sq = jnp.sum(weight * weight)
    update_sq = jnp.sum(direction * direction)
    row = lax.broadcasted_iota(jnp.int32, (8, 128), 0)
    sums_out[...] = jnp.where(row == 0, weight_sq, update_sq)


def optimizer(ga, gb, w, m, v):
    shape = jax.ShapeDtypeStruct((ROWS, COLS), f32)
    return pl.pallas_call(
        optimizer_kernel,
        out_shape=[
            shape,
            shape,
            shape,
            jax.ShapeDtypeStruct((2, ROWS_A, COLS), bf16),
            jax.ShapeDtypeStruct((2, ROWS_B, COLS), bf16),
            jax.ShapeDtypeStruct((8, 128), f32),
        ],
        compiler_params=pltpu.CompilerParams(vmem_limit_bytes=32 << 20),
        name="optimizer",
    )(ga, gb, w, m, v)


def apply_kernel(place_ref, sums_ref, a0, a1, a2, a3, b_ref, a_out, b_out):
    sums = jnp.sum(sums_ref[...], axis=0)
    rate = learn_rate * (jnp.sqrt(sums[0:1, 0:1]) / jnp.sqrt(sums[1:2, 0:1]))
    for k, ref in enumerate((a0, a1, a2, a3)):
        new = ref[1].astype(f32) - rate * ref[0].astype(f32)
        a_out[place_ref[k]] = new.astype(bf16)
    for z in range(NZ):
        new = b_ref[z, 1].astype(f32) - rate * b_ref[z, 0].astype(f32)
        b_out[z] = new.astype(bf16)


def apply_step(place, sums, pieces, gathered):
    vmem = pl.BlockSpec(memory_space=pltpu.VMEM)
    return pl.pallas_call(
        apply_kernel,
        in_specs=[pl.BlockSpec(memory_space=pltpu.SMEM)] + [vmem] * 6,
        out_specs=[vmem, vmem],
        out_shape=[
            jax.ShapeDtypeStruct((NX, ROWS_A, COLS), bf16),
            jax.ShapeDtypeStruct((NZ, ROWS_B, COLS), bf16),
        ],
        compiler_params=pltpu.CompilerParams(vmem_limit_bytes=32 << 20),
        name="apply",
    )(place, sums, *pieces, gathered)


def join_kernel(place_ref, a_ref, b0, b1, b2, b3, b4, out_ref):
    step, half = pl.program_id(0), pl.program_id(1)
    for z in range(a_ref.shape[0]):
        out_ref[0, z, 0:ROWS_A, :] = a_ref[z, 0]
    for k, ref in enumerate((b0, b1, b2)):

        @pl.when(step == k)
        def _(ref=ref):
            out_ref[0, :, ROWS_A:ROWS, :] = ref[...]

    for k, ref in enumerate((b3, b4)):

        @pl.when((step == 3) & (half == k))
        def _(ref=ref):
            out_ref[0, :, ROWS_A:ROWS, :] = ref[...]


def join(place, a_full, own, before, after, far_lo, far_hi):
    half = NZ // 2

    def b_spec(k):
        return pl.BlockSpec(
            (half, ROWS_B, COLS),
            lambda o, h, place: (jnp.where(o < k, 0, jnp.where(o > k, 1, h)), 0, 0),
        )

    whole = pl.BlockSpec((half, ROWS_B, COLS), lambda o, h, place: (0, 0, 0))
    return pl.pallas_call(
        join_kernel,
        grid_spec=pltpu.PrefetchScalarGridSpec(
            num_scalar_prefetch=1,
            grid=(NX, 2),
            in_specs=[
                pl.BlockSpec((half, 1, ROWS_A, COLS), lambda o, h, place: (h, place[o], 0, 0)),
                b_spec(0),
                b_spec(1),
                b_spec(2),
                whole,
                whole,
            ],
            out_specs=pl.BlockSpec(
                (1, half, ROWS, COLS), lambda o, h, place: (place[o], h, 0, 0)
            ),
        ),
        out_shape=jax.ShapeDtypeStruct((NX, NZ, ROWS, COLS), bf16),
        compiler_params=pltpu.CompilerParams(vmem_limit_bytes=48 << 20),
        cost_estimate=pl.CostEstimate(flops=0, bytes_accessed=13 << 20, transcendentals=0),
        name="join",
    )(place, a_full, own, before, after, far_lo, far_hi)


def shift(value, axis, size, by):
    return lax.ppermute(value, axis, [(i, (i + by) % size) for i in range(size)])


def spread(sums, axes, size):
    wide = jnp.broadcast_to(sums[None], (size,) + sums.shape)
    return lax.all_to_all(wide, axes, 0, 0, tiled=True)


def body(x, q, k, v, g, w, m, s):
    packed = pack(q[0], k[0], v[0], g[0])
    heads = lax.all_to_all(packed, ("y", "core"), 0, 0, tiled=True).reshape(LENGTH, PACKED)
    x_full = lax.all_gather(x[0], ("y", "core"), axis=0, tiled=True)
    grouped = attention(heads)

    part_a = project(grouped, x_full, 0, COLS_A, True)
    part_b = project(grouped, x_full, COLS_A, COLS, False)
    part_a = lax.psum_scatter(part_a, "z", scatter_dimension=0, tiled=True)[0]
    part_b = lax.all_to_all(part_b, "x", 0, 0, tiled=True)
    part_b = jnp.sum(part_b.astype(f32), axis=0).astype(bf16)
    part_b = lax.all_to_all(part_b, "z", 0, 0, tiled=True)
    part_a = lax.all_to_all(part_a, "x", 0, 0, tiled=True)

    first_new, second_new, direction, mine_a, mine_b, sums = optimizer(part_a, part_b, w, m, s)
    at_x = lax.axis_index("x")
    place = jnp.stack([at_x, (at_x + 3) % NX, (at_x + 1) % NX, (at_x + 2) % NX]).astype(jnp.int32)
    pieces = (
        mine_a,
        shift(mine_a, "x", NX, 1),
        shift(mine_a, "x", NX, -1),
        shift(mine_a, "x", NX, 2),
    )
    gathered_b = lax.all_gather(mine_b, "z", axis=0, tiled=False)
    sums = spread(jnp.sum(spread(sums, ("y", "core"), 8), axis=0), ("x", "z"), 32)
    new_a, new_b = apply_step(place, sums, pieces, gathered_b)
    full_a = lax.all_gather(new_a, "z", axis=0, tiled=False)
    before, after = shift(new_b, "x", NX, 1), shift(new_b, "x", NX, -1)
    far_lo = shift(before[: NZ // 2], "x", NX, 1)
    far_hi = shift(after[NZ // 2 :], "x", NX, -1)
    new_weights = join(place, full_a, new_b, before, after, far_lo, far_hi)

    total = jnp.sum(sums, axis=0)
    lamb_update = (jnp.sqrt(total[0, 0]) / jnp.sqrt(total[1, 0])) * direction
    return first_new, second_new, lamb_update, new_weights.reshape(WIDTH, COLS)


def solution(mesh):
    fine = Mesh(mesh.devices.reshape(NX, NZ, NY, NCORE), ("x", "z", "y", "core"))
    dp, ctx = ("x", "z"), ("y", "core")
    seq = P(dp, ctx, None)
    mat = P(dp, ctx)
    return jax.shard_map(
        body,
        mesh=fine,
        in_specs=(seq, seq, seq, seq, seq, mat, mat, mat),
        out_specs=(mat, mat, mat, P(None, ctx)),
        check_vma=False,
    )
```

```python
import jax
import jax.numpy as jnp
from jax import lax
from jax.experimental import pallas as pl
from jax.experimental.pallas import tpu as pltpu
from jax.sharding import Mesh
from jax.sharding import PartitionSpec as P

HEAD_DIM = 128
STEP = 100
GROUP = 4
NX, NZ, NY, NCORE = 4, 8, 4, 2
LENGTH = 1024
COLS = 768
WIDTH = 4096
ROWS = 128
PACKED = 1280
BLOCK = 256
COLS_A = 480
COLS_B = COLS - COLS_A
ROWS_A = 64
ROWS_B = ROWS - ROWS_A

beta_first = 0.9
beta_second = 0.999
adam_epsilon = 1e-06
decay_rate = 0.01
learn_rate = 0.01
masked_score = -1e30
score_scale = HEAD_DIM ** (-0.5)
LOG2E = 1.4426950408889634

f32 = jnp.float32
bf16 = jnp.bfloat16


def dot(a, b, ca, cb):
    return lax.dot_general(a, b, (((ca,), (cb,)), ((), ())), preferred_element_type=f32)


def pack_kernel(q_ref, k_ref, v_ref, g_ref, out_ref):
    for c in range(out_ref.shape[0]):
        out_ref[c, :, 0:512] = q_ref[:, c * 512 : (c + 1) * 512]
        out_ref[c, :, 512:640] = k_ref[:, c * 128 : (c + 1) * 128]
        out_ref[c, :, 640:768] = v_ref[:, c * 128 : (c + 1) * 128]
        out_ref[c, :, 768:1280] = g_ref[:, c * 512 : (c + 1) * 512]


def pack(q, k, v, g):
    rows = q.shape[0]
    each = 4
    return pl.pallas_call(
        pack_kernel,
        grid=(8 // each,),
        in_specs=[
            pl.BlockSpec((rows, 512 * each), lambda c: (0, c)),
            pl.BlockSpec((rows, 128 * each), lambda c: (0, c)),
            pl.BlockSpec((rows, 128 * each), lambda c: (0, c)),
            pl.BlockSpec((rows, 512 * each), lambda c: (0, c)),
        ],
        out_specs=pl.BlockSpec((each, rows, PACKED), lambda c: (c, 0, 0)),
        out_shape=jax.ShapeDtypeStruct((8, rows, PACKED), bf16),
        cost_estimate=pl.CostEstimate(flops=0, bytes_accessed=5 << 20, transcendentals=0),
        name="pack",
    )(q, k, v, g)


def attention_kernel(q_ref, k_ref, v_ref, g_ref, out_ref, kt_ref, dk_acc, dv_acc):
    head = pl.program_id(0)

    @pl.when(head == 0)
    def _():
        kt_ref[...] = k_ref[...].T
        dk_acc[...] = jnp.zeros_like(dk_acc)
        dv_acc[...] = jnp.zeros_like(dv_acc)

    key_pos = lax.broadcasted_iota(jnp.int32, (BLOCK, BLOCK), 0)
    query_pos = lax.broadcasted_iota(jnp.int32, (BLOCK, BLOCK), 1)
    allowed = key_pos <= query_pos
    for i in range(LENGTH // BLOCK):
        lo, hi = i * BLOCK, (i + 1) * BLOCK
        q = q_ref[lo:hi, :]
        g = g_ref[lo:hi, :]
        scores = dot(k_ref[:hi, :], q, 1, 1)
        diag = jnp.where(allowed, scores[lo:hi, :], masked_score)
        scores = diag if i == 0 else jnp.concatenate([scores[:lo, :], diag], axis=0)
        top = jnp.max(scores, axis=0, keepdims=True)
        weights = jnp.exp2((scores - top) * (score_scale * LOG2E))
        probs = weights * (1.0 / jnp.sum(weights, axis=0, keepdims=True))
        probs_b = probs.astype(bf16)
        prob_grad = dot(v_ref[:hi, :], g, 1, 1)
        row_delta = jnp.sum(probs_b.astype(f32) * prob_grad, axis=0, keepdims=True)
        dscore = (probs * (prob_grad - row_delta)).astype(bf16)
        dq_t = dot(kt_ref[:, :hi], dscore, 1, 0) * score_scale
        out_ref[pl.ds(pl.multiple_of(head * 128, 128), 128), lo:hi] = dq_t.astype(bf16)
        dk_acc[:hi, :] += dot(dscore, q, 1, 0)
        dv_acc[:hi, :] += dot(probs_b, g, 1, 0)

    @pl.when(head == GROUP - 1)
    def _():
        out_ref[512:640, :] = (dk_acc[...] * score_scale).astype(bf16).T
        out_ref[640:768, :] = dv_acc[...].astype(bf16).T


def attention(packed):
    return pl.pallas_call(
        attention_kernel,
        grid=(GROUP,),
        in_specs=[
            pl.BlockSpec((LENGTH, 128), lambda h: (0, h)),
            pl.BlockSpec((LENGTH, 128), lambda h: (0, 4)),
            pl.BlockSpec((LENGTH, 128), lambda h: (0, 5)),
            pl.BlockSpec((LENGTH, 128), lambda h: (0, 6 + h)),
        ],
        out_specs=pl.BlockSpec((COLS, LENGTH), lambda h: (0, 0)),
        out_shape=jax.ShapeDtypeStruct((COLS, LENGTH), bf16),
        scratch_shapes=[
            pltpu.VMEM((128, LENGTH), bf16),
            pltpu.VMEM((LENGTH, 128), f32),
            pltpu.VMEM((LENGTH, 128), f32),
        ],
        compiler_params=pltpu.CompilerParams(vmem_limit_bytes=48 << 20),
        cost_estimate=pl.CostEstimate(
            flops=4 << 30, bytes_accessed=5 << 20, transcendentals=4 << 20
        ),
        name="attention_backward",
    )(packed, packed, packed, packed)


def project_kernel(grouped_ref, x_ref, a_ref, b_ref):
    res = dot(grouped_ref[...], x_ref[...], 1, 0).astype(bf16)
    for i in range(a_ref.shape[0]):
        a_ref[i, 0] = res[:COLS_A, i * ROWS : (i + 1) * ROWS]
        b_ref[0, i] = res[COLS_A:, i * ROWS : (i + 1) * ROWS]


def project(grouped, x):
    tile = 4
    return pl.pallas_call(
        project_kernel,
        grid=(NX, NZ // tile),
        in_specs=[
            pl.BlockSpec((COLS, LENGTH), lambda x, z: (0, 0)),
            pl.BlockSpec((LENGTH, ROWS * tile), lambda x, z: (0, x * (NZ // tile) + z)),
        ],
        out_specs=[
            pl.BlockSpec((tile, 1, COLS_A, ROWS), lambda x, z: (z, x, 0, 0)),
            pl.BlockSpec((1, tile, COLS_B, ROWS), lambda x, z: (x, z, 0, 0)),
        ],
        out_shape=[
            jax.ShapeDtypeStruct((NZ, NX, COLS_A, ROWS), bf16),
            jax.ShapeDtypeStruct((NX, NZ, COLS_B, ROWS), bf16),
        ],
        compiler_params=pltpu.CompilerParams(vmem_limit_bytes=60 << 20),
        cost_estimate=pl.CostEstimate(flops=6 << 30, bytes_accessed=16 << 20, transcendentals=0),
        name="project",
    )(grouped, x)


def optimizer_kernel(ga_ref, gb_ref, w_ref, m_ref, v_ref, m_out, v_out, dir_out, a_out, b_out, sums_out):
    grad_a = jnp.sum(ga_ref[...].astype(f32), axis=0)
    grad_b = jnp.sum(gb_ref[...].astype(f32), axis=0)
    gradient = jnp.concatenate([grad_a, grad_b], axis=0).T
    weight = w_ref[...]
    first_new = beta_first * m_ref[...] + (1.0 - beta_first) * gradient
    second_new = beta_second * v_ref[...] + (1.0 - beta_second) * gradient * gradient
    corr_first = 1.0 - beta_first**STEP
    corr_second = 1.0 - beta_second**STEP
    direction = (
        first_new / corr_first / (jnp.sqrt(second_new / corr_second) + adam_epsilon)
        + decay_rate * weight
    )
    m_out[...] = first_new
    v_out[...] = second_new
    dir_out[...] = direction
    a_out[0] = direction[:ROWS_A].astype(bf16)
    a_out[1] = weight[:ROWS_A].astype(bf16)
    b_out[0] = direction[ROWS_A:].astype(bf16)
    b_out[1] = weight[ROWS_A:].astype(bf16)
    weight_sq = jnp.sum(weight * weight)
    update_sq = jnp.sum(direction * direction)
    row = lax.broadcasted_iota(jnp.int32, (8, 128), 0)
    sums_out[...] = jnp.where(row == 0, weight_sq, update_sq)


def optimizer(ga, gb, w, m, v):
    shape = jax.ShapeDtypeStruct((ROWS, COLS), f32)
    return pl.pallas_call(
        optimizer_kernel,
        out_shape=[
            shape,
            shape,
            shape,
            jax.ShapeDtypeStruct((2, ROWS_A, COLS), bf16),
            jax.ShapeDtypeStruct((2, ROWS_B, COLS), bf16),
            jax.ShapeDtypeStruct((8, 128), f32),
        ],
        compiler_params=pltpu.CompilerParams(vmem_limit_bytes=32 << 20),
        name="optimizer",
    )(ga, gb, w, m, v)


def apply_kernel(place_ref, sums_ref, a0, a1, a2, a3, b_ref, a_out, b_out):
    sums = jnp.sum(sums_ref[...], axis=0)
    rate = learn_rate * (jnp.sqrt(sums[0:1, 0:1]) / jnp.sqrt(sums[1:2, 0:1]))
    for k, ref in enumerate((a0, a1, a2, a3)):
        new = ref[1].astype(f32) - rate * ref[0].astype(f32)
        a_out[place_ref[k]] = new.astype(bf16)
    for z in range(NZ):
        new = b_ref[z, 1].astype(f32) - rate * b_ref[z, 0].astype(f32)
        b_out[z] = new.astype(bf16)


def apply_step(place, sums, pieces, gathered):
    vmem = pl.BlockSpec(memory_space=pltpu.VMEM)
    return pl.pallas_call(
        apply_kernel,
        in_specs=[pl.BlockSpec(memory_space=pltpu.SMEM)] + [vmem] * 6,
        out_specs=[vmem, vmem],
        out_shape=[
            jax.ShapeDtypeStruct((NX, ROWS_A, COLS), bf16),
            jax.ShapeDtypeStruct((NZ, ROWS_B, COLS), bf16),
        ],
        compiler_params=pltpu.CompilerParams(vmem_limit_bytes=32 << 20),
        name="apply",
    )(place, sums, *pieces, gathered)


FULL = (NX, NZ, ROWS, COLS)


def join_x_kernel(place_ref, b0, b1, b2, b3, b4, out_ref):
    step, half = pl.program_id(0), pl.program_id(1)
    for k, ref in enumerate((b0, b1, b2)):

        @pl.when(step == k)
        def _(ref=ref):
            out_ref[0] = ref[...]

    for k, ref in enumerate((b3, b4)):

        @pl.when((step == 3) & (half == k))
        def _(ref=ref):
            out_ref[0] = ref[...]


def join_x(place, own, before, after, far_lo, far_hi):
    half = NZ // 2

    def b_spec(k):
        return pl.BlockSpec(
            (half, ROWS_B, COLS),
            lambda o, h, place: (jnp.where(o < k, 0, jnp.where(o > k, 1, h)), 0, 0),
        )

    whole = pl.BlockSpec((half, ROWS_B, COLS), lambda o, h, place: (0, 0, 0))
    return pl.pallas_call(
        join_x_kernel,
        grid_spec=pltpu.PrefetchScalarGridSpec(
            num_scalar_prefetch=1,
            grid=(NX, 2),
            in_specs=[b_spec(0), b_spec(1), b_spec(2), whole, whole],
            out_specs=pl.BlockSpec(
                (1, half, ROWS_B, COLS),
                lambda o, h, place: (place[o], h, ROWS_A // ROWS_B, 0),
            ),
        ),
        out_shape=jax.ShapeDtypeStruct(FULL, bf16),
        compiler_params=pltpu.CompilerParams(vmem_limit_bytes=48 << 20),
        cost_estimate=pl.CostEstimate(flops=0, bytes_accessed=7 << 20, transcendentals=0),
        name="join_x",
    )(place, own, before, after, far_lo, far_hi)


def join_sc_kernel(base_ref, a_ref, out_ref):
    out_ref[0] = a_ref[:, 0]


def join_sc(base, full):
    return pl.pallas_call(
        join_sc_kernel,
        grid=(NX,),
        in_specs=[
            pl.BlockSpec(memory_space=pl.ANY),
            pl.BlockSpec((NZ, 1, ROWS_A, COLS), lambda x: (0, x, 0, 0)),
        ],
        out_specs=pl.BlockSpec((1, NZ, ROWS_A, COLS), lambda x: (x, 0, 0, 0)),
        out_shape=jax.ShapeDtypeStruct(FULL, bf16),
        input_output_aliases={0: 0},
        compiler_params=pltpu.CompilerParams(vmem_limit_bytes=48 << 20),
        cost_estimate=pl.CostEstimate(flops=0, bytes_accessed=4 << 20, transcendentals=0),
        name="join_sc",
    )(base, full)


def shift(value, axis, size, by):
    return lax.ppermute(value, axis, [(i, (i + by) % size) for i in range(size)])


def spread(sums, axes, size):
    wide = jnp.broadcast_to(sums[None], (size,) + sums.shape)
    return lax.all_to_all(wide, axes, 0, 0, tiled=True)


def body(x, q, k, v, g, w, m, s):
    packed = pack(q[0], k[0], v[0], g[0])
    heads = lax.all_to_all(packed, ("y", "core"), 0, 0, tiled=True).reshape(LENGTH, PACKED)
    x_full = lax.all_gather(x[0], ("y", "core"), axis=0, tiled=True)
    grouped = attention(heads)

    part_a, part_b = project(grouped, x_full)
    part_a = lax.psum_scatter(part_a, "z", scatter_dimension=0, tiled=True)[0]
    part_b = lax.all_to_all(part_b, "x", 0, 0, tiled=True)
    part_b = jnp.sum(part_b.astype(f32), axis=0).astype(bf16)
    part_b = lax.all_to_all(part_b, "z", 0, 0, tiled=True)
    part_a = lax.all_to_all(part_a, "x", 0, 0, tiled=True)

    first_new, second_new, direction, mine_a, mine_b, sums = optimizer(part_a, part_b, w, m, s)
    at_x = lax.axis_index("x")
    place = jnp.stack([at_x, (at_x + 3) % NX, (at_x + 1) % NX, (at_x + 2) % NX]).astype(jnp.int32)
    pieces = (
        mine_a,
        shift(mine_a, "x", NX, 1),
        shift(mine_a, "x", NX, -1),
        shift(mine_a, "x", NX, 2),
    )
    gathered_b = lax.all_gather(mine_b, "z", axis=0, tiled=False)
    sums = spread(jnp.sum(spread(sums, ("y", "core"), 8), axis=0), ("x", "z"), 32)
    new_a, new_b = apply_step(place, sums, pieces, gathered_b)
    full_a = lax.all_gather(new_a, "z", axis=0, tiled=False)
    before, after = shift(new_b, "x", NX, 1), shift(new_b, "x", NX, -1)
    far_lo = shift(before[: NZ // 2], "x", NX, 1)
    far_hi = shift(after[NZ // 2 :], "x", NX, -1)
    new_weights = join_x(place, new_b, before, after, far_lo, far_hi)
    new_weights = join_sc(new_weights, full_a)

    total = jnp.sum(sums, axis=0)
    lamb_update = (jnp.sqrt(total[0, 0]) / jnp.sqrt(total[1, 0])) * direction
    return first_new, second_new, lamb_update, new_weights.reshape(WIDTH, COLS)


def solution(mesh):
    fine = Mesh(mesh.devices.reshape(NX, NZ, NY, NCORE), ("x", "z", "y", "core"))
    dp, ctx = ("x", "z"), ("y", "core")
    seq = P(dp, ctx, None)
    mat = P(dp, ctx)
    return jax.shard_map(
        body,
        mesh=fine,
        in_specs=(seq, seq, seq, seq, seq, mat, mat, mat),
        out_specs=(mat, mat, mat, P(None, ctx)),
        check_vma=False,
    )
```

```python
import jax
import jax.numpy as jnp
from jax import lax
from jax.experimental import pallas as pl
from jax.experimental.pallas import tpu as pltpu
from jax.sharding import Mesh
from jax.sharding import PartitionSpec as P

HEAD_DIM = 128
STEP = 100
GROUP = 4
NX, NZ, NY, NCORE = 4, 8, 4, 2
LENGTH = 1024
COLS = 768
WIDTH = 4096
ROWS = 128
PACKED = 1280
BLOCK = 256
PART_A = 80
PART_B = ROWS - PART_A
TILE = 4
ROWS_A = 64
ROWS_B = ROWS - ROWS_A

beta_first = 0.9
beta_second = 0.999
adam_epsilon = 1e-06
decay_rate = 0.01
learn_rate = 0.01
masked_score = -1e30
score_scale = HEAD_DIM ** (-0.5)
LOG2E = 1.4426950408889634

f32 = jnp.float32
bf16 = jnp.bfloat16


def dot(a, b, ca, cb):
    return lax.dot_general(a, b, (((ca,), (cb,)), ((), ())), preferred_element_type=f32)


def pack_kernel(q_ref, k_ref, v_ref, g_ref, out_ref):
    for c in range(out_ref.shape[0]):
        out_ref[c, :, 0:512] = q_ref[:, c * 512 : (c + 1) * 512]
        out_ref[c, :, 512:640] = k_ref[:, c * 128 : (c + 1) * 128]
        out_ref[c, :, 640:768] = v_ref[:, c * 128 : (c + 1) * 128]
        out_ref[c, :, 768:1280] = g_ref[:, c * 512 : (c + 1) * 512]


def pack(q, k, v, g):
    rows = q.shape[0]
    each = 4
    return pl.pallas_call(
        pack_kernel,
        grid=(8 // each,),
        in_specs=[
            pl.BlockSpec((rows, 512 * each), lambda c: (0, c)),
            pl.BlockSpec((rows, 128 * each), lambda c: (0, c)),
            pl.BlockSpec((rows, 128 * each), lambda c: (0, c)),
            pl.BlockSpec((rows, 512 * each), lambda c: (0, c)),
        ],
        out_specs=pl.BlockSpec((each, rows, PACKED), lambda c: (c, 0, 0)),
        out_shape=jax.ShapeDtypeStruct((8, rows, PACKED), bf16),
        cost_estimate=pl.CostEstimate(flops=0, bytes_accessed=5 << 20, transcendentals=0),
        name="pack",
    )(q, k, v, g)


def turn_kernel(x_ref, a_ref, b_ref):
    for i in range(x_ref.shape[1] // ROWS):
        tile = x_ref[:, i * ROWS : (i + 1) * ROWS].T
        a_ref[i] = tile[:PART_A]
        b_ref[i] = tile[PART_A:]


def turn(x):
    tokens = x.shape[0]
    each = 16
    return pl.pallas_call(
        turn_kernel,
        grid=(NX * NZ // each,),
        in_specs=[pl.BlockSpec((tokens, ROWS * each), lambda i: (0, i))],
        out_specs=[
            pl.BlockSpec((each, PART_A, tokens), lambda i: (i, 0, 0)),
            pl.BlockSpec((each, PART_B, tokens), lambda i: (i, 0, 0)),
        ],
        out_shape=[
            jax.ShapeDtypeStruct((NX * NZ, PART_A, tokens), bf16),
            jax.ShapeDtypeStruct((NX * NZ, PART_B, tokens), bf16),
        ],
        cost_estimate=pl.CostEstimate(flops=0, bytes_accessed=2 << 20, transcendentals=0),
        name="turn",
    )(x)


def attention_kernel(q_ref, k_ref, v_ref, g_ref, out_ref, kt_ref, dk_acc, dv_acc):
    head = pl.program_id(0)

    @pl.when(head == 0)
    def _():
        kt_ref[...] = k_ref[...].T
        dk_acc[...] = jnp.zeros_like(dk_acc)
        dv_acc[...] = jnp.zeros_like(dv_acc)

    key_pos = lax.broadcasted_iota(jnp.int32, (BLOCK, BLOCK), 0)
    query_pos = lax.broadcasted_iota(jnp.int32, (BLOCK, BLOCK), 1)
    allowed = key_pos <= query_pos
    for i in range(LENGTH // BLOCK):
        lo, hi = i * BLOCK, (i + 1) * BLOCK
        q = q_ref[lo:hi, :]
        g = g_ref[lo:hi, :]
        scores = dot(k_ref[:hi, :], q, 1, 1)
        diag = jnp.where(allowed, scores[lo:hi, :], masked_score)
        scores = diag if i == 0 else jnp.concatenate([scores[:lo, :], diag], axis=0)
        top = jnp.max(scores, axis=0, keepdims=True)
        weights = jnp.exp2((scores - top) * (score_scale * LOG2E))
        probs = weights * (1.0 / jnp.sum(weights, axis=0, keepdims=True))
        probs_b = probs.astype(bf16)
        prob_grad = dot(v_ref[:hi, :], g, 1, 1)
        row_delta = jnp.sum(probs_b.astype(f32) * prob_grad, axis=0, keepdims=True)
        dscore = (probs * (prob_grad - row_delta)).astype(bf16)
        dq_t = dot(kt_ref[:, :hi], dscore, 1, 0) * score_scale
        out_ref[lo:hi, pl.ds(pl.multiple_of(head * 128, 128), 128)] = dq_t.astype(bf16).T
        dk_acc[:hi, :] += dot(dscore, q, 1, 0)
        dv_acc[:hi, :] += dot(probs_b, g, 1, 0)

    @pl.when(head == GROUP - 1)
    def _():
        out_ref[:, 512:640] = (dk_acc[...] * score_scale).astype(bf16)
        out_ref[:, 640:768] = dv_acc[...].astype(bf16)


def attention(packed):
    return pl.pallas_call(
        attention_kernel,
        grid=(GROUP,),
        in_specs=[
            pl.BlockSpec((LENGTH, 128), lambda h: (0, h)),
            pl.BlockSpec((LENGTH, 128), lambda h: (0, 4)),
            pl.BlockSpec((LENGTH, 128), lambda h: (0, 5)),
            pl.BlockSpec((LENGTH, 128), lambda h: (0, 6 + h)),
        ],
        out_specs=pl.BlockSpec((LENGTH, COLS), lambda h: (0, 0)),
        out_shape=jax.ShapeDtypeStruct((LENGTH, COLS), bf16),
        scratch_shapes=[
            pltpu.VMEM((128, LENGTH), bf16),
            pltpu.VMEM((LENGTH, 128), f32),
            pltpu.VMEM((LENGTH, 128), f32),
        ],
        compiler_params=pltpu.CompilerParams(vmem_limit_bytes=48 << 20),
        cost_estimate=pl.CostEstimate(
            flops=4 << 30, bytes_accessed=5 << 20, transcendentals=4 << 20
        ),
        name="attention_backward",
    )(packed, packed, packed, packed)


def project_a_kernel(at_x, grouped_ref, x_ref, out_ref):
    rows = jnp.concatenate(
        [x_ref[t].reshape(TILE * PART_A, ROWS) for t in range(x_ref.shape[0])], axis=1
    )
    res = dot(rows, grouped_ref[...], 1, 0).astype(bf16)
    out_ref[...] = res.reshape(out_ref.shape)


def project_a(at_x, grouped, x):
    per = NZ // TILE
    return pl.pallas_call(
        project_a_kernel,
        grid_spec=pltpu.PrefetchScalarGridSpec(
            num_scalar_prefetch=1,
            grid=(NX, per),
            in_specs=[
                pl.BlockSpec((LENGTH, COLS), lambda x, z, at_x: (0, 0)),
                pl.BlockSpec((8, TILE, PART_A, ROWS), lambda x, z, at_x: (0, x * per + z, 0, 0)),
            ],
            out_specs=pl.BlockSpec(
                (TILE, 1, PART_A, COLS),
                lambda x, z, at_x: (z, lax.rem(x - at_x[0] + NX, NX), 0, 0),
            ),
        ),
        out_shape=jax.ShapeDtypeStruct((NZ, NX, PART_A, COLS), bf16),
        compiler_params=pltpu.CompilerParams(vmem_limit_bytes=60 << 20),
        cost_estimate=pl.CostEstimate(
            flops=2 * LENGTH * COLS * WIDTH * PART_A // ROWS,
            bytes_accessed=10 << 20,
            transcendentals=0,
        ),
        name="project_a",
    )(at_x, grouped, x)


def project_b_kernel(offsets, grouped_ref, *refs):
    *pieces, out_ref, ordered_ref = refs
    step = pl.program_id(0) * (NZ // TILE) + pl.program_id(1)

    @pl.when(step == 0)
    def _():
        for k in range(8):
            start = pl.multiple_of(offsets[k], ROWS)
            ordered_ref[k * ROWS : (k + 1) * ROWS, :] = grouped_ref[pl.ds(start, ROWS), :]

    flat = [ref[...].reshape(TILE * PART_B, ROWS) for ref in pieces]
    early = step < NX * NZ // TILE // 2
    far = [jnp.where(early, flat[6], flat[8]), jnp.where(early, flat[7], flat[9])]
    rows = jnp.concatenate(flat[:6] + far, axis=1)
    res = dot(rows, ordered_ref[...], 1, 0).astype(bf16)
    out_ref[...] = res.reshape(out_ref.shape)


def project_b(offsets, grouped, pieces):
    per = NZ // TILE
    half = NX * NZ // TILE // 2
    block = (TILE, PART_B, ROWS)
    return pl.pallas_call(
        project_b_kernel,
        grid_spec=pltpu.PrefetchScalarGridSpec(
            num_scalar_prefetch=1,
            grid=(NX, per),
            in_specs=[
                pl.BlockSpec((LENGTH, COLS), lambda x, z, offsets: (0, 0)),
                *[pl.BlockSpec(block, lambda x, z, offsets: (x * per + z, 0, 0))] * 6,
                *[
                    pl.BlockSpec(
                        block, lambda x, z, offsets: (jnp.minimum(x * per + z, half - 1), 0, 0)
                    )
                ]
                * 2,
                *[
                    pl.BlockSpec(
                        block, lambda x, z, offsets: (jnp.maximum(x * per + z - half, 0), 0, 0)
                    )
                ]
                * 2,
            ],
            out_specs=pl.BlockSpec((1, TILE, PART_B, COLS), lambda x, z, offsets: (x, z, 0, 0)),
            scratch_shapes=[pltpu.VMEM((LENGTH, COLS), bf16)],
        ),
        out_shape=jax.ShapeDtypeStruct((NX, NZ, PART_B, COLS), bf16),
        compiler_params=pltpu.CompilerParams(vmem_limit_bytes=60 << 20),
        cost_estimate=pl.CostEstimate(
            flops=2 * LENGTH * COLS * WIDTH * PART_B // ROWS,
            bytes_accessed=8 << 20,
            transcendentals=0,
        ),
        name="project_b",
    )(offsets, grouped, *pieces)


def optimizer_kernel(ga0, ga1, ga2, ga3, gb_ref, w_ref, m_ref, v_ref, m_out, v_out, dir_out, a_out, b_out, sums_out):
    grad_a = ga0[...].astype(f32) + ga1[...].astype(f32)
    grad_a = grad_a + ga2[...].astype(f32) + ga3[...].astype(f32)
    grad_b = jnp.sum(gb_ref[...].astype(f32), axis=0)
    gradient = jnp.concatenate([grad_a, grad_b], axis=0)
    weight = w_ref[...]
    first_new = beta_first * m_ref[...] + (1.0 - beta_first) * gradient
    second_new = beta_second * v_ref[...] + (1.0 - beta_second) * gradient * gradient
    corr_first = 1.0 - beta_first**STEP
    corr_second = 1.0 - beta_second**STEP
    direction = (
        first_new / corr_first / (jnp.sqrt(second_new / corr_second) + adam_epsilon)
        + decay_rate * weight
    )
    m_out[...] = first_new
    v_out[...] = second_new
    dir_out[...] = direction
    a_out[0] = direction[:ROWS_A].astype(bf16)
    a_out[1] = weight[:ROWS_A].astype(bf16)
    b_out[0] = direction[ROWS_A:].astype(bf16)
    b_out[1] = weight[ROWS_A:].astype(bf16)
    weight_sq = jnp.sum(weight * weight)
    update_sq = jnp.sum(direction * direction)
    row = lax.broadcasted_iota(jnp.int32, (8, 128), 0)
    sums_out[...] = jnp.where(row == 0, weight_sq, update_sq)


def optimizer(ga, gb, w, m, v):
    shape = jax.ShapeDtypeStruct((ROWS, COLS), f32)
    return pl.pallas_call(
        optimizer_kernel,
        out_shape=[
            shape,
            shape,
            shape,
            jax.ShapeDtypeStruct((2, ROWS_A, COLS), bf16),
            jax.ShapeDtypeStruct((2, ROWS_B, COLS), bf16),
            jax.ShapeDtypeStruct((8, 128), f32),
        ],
        compiler_params=pltpu.CompilerParams(vmem_limit_bytes=32 << 20),
        name="optimizer",
    )(*ga, gb, w, m, v)


def apply_kernel(place_ref, sums_ref, a0, a1, a2, a3, b_ref, a_out, b_out):
    sums = jnp.sum(sums_ref[...], axis=0)
    rate = learn_rate * (jnp.sqrt(sums[0:1, 0:1]) / jnp.sqrt(sums[1:2, 0:1]))
    for k, ref in enumerate((a0, a1, a2, a3)):
        new = ref[1].astype(f32) - rate * ref[0].astype(f32)
        a_out[place_ref[k]] = new.astype(bf16)
    for z in range(NZ):
        new = b_ref[z, 1].astype(f32) - rate * b_ref[z, 0].astype(f32)
        b_out[z] = new.astype(bf16)


def apply_step(place, sums, pieces, gathered):
    vmem = pl.BlockSpec(memory_space=pltpu.VMEM)
    return pl.pallas_call(
        apply_kernel,
        in_specs=[pl.BlockSpec(memory_space=pltpu.SMEM)] + [vmem] * 6,
        out_specs=[vmem, vmem],
        out_shape=[
            jax.ShapeDtypeStruct((NX, ROWS_A, COLS), bf16),
            jax.ShapeDtypeStruct((NZ, ROWS_B, COLS), bf16),
        ],
        compiler_params=pltpu.CompilerParams(vmem_limit_bytes=32 << 20),
        name="apply",
    )(place, sums, *pieces, gathered)


FULL = (NX, NZ, ROWS, COLS)


def join_x_kernel(place_ref, b0, b1, b2, b3, b4, out_ref):
    step, half = pl.program_id(0), pl.program_id(1)
    for k, ref in enumerate((b0, b1, b2)):

        @pl.when(step == k)
        def _(ref=ref):
            out_ref[0] = ref[...]

    for k, ref in enumerate((b3, b4)):

        @pl.when((step == 3) & (half == k))
        def _(ref=ref):
            out_ref[0] = ref[...]


def join_x(place, own, before, after, far_lo, far_hi):
    half = NZ // 2

    def b_spec(k):
        return pl.BlockSpec(
            (half, ROWS_B, COLS),
            lambda o, h, place: (jnp.where(o < k, 0, jnp.where(o > k, 1, h)), 0, 0),
        )

    whole = pl.BlockSpec((half, ROWS_B, COLS), lambda o, h, place: (0, 0, 0))
    return pl.pallas_call(
        join_x_kernel,
        grid_spec=pltpu.PrefetchScalarGridSpec(
            num_scalar_prefetch=1,
            grid=(NX, 2),
            in_specs=[b_spec(0), b_spec(1), b_spec(2), whole, whole],
            out_specs=pl.BlockSpec(
                (1, half, ROWS_B, COLS),
                lambda o, h, place: (place[o], h, ROWS_A // ROWS_B, 0),
            ),
        ),
        out_shape=jax.ShapeDtypeStruct(FULL, bf16),
        compiler_params=pltpu.CompilerParams(vmem_limit_bytes=48 << 20),
        cost_estimate=pl.CostEstimate(flops=0, bytes_accessed=7 << 20, transcendentals=0),
        name="join_x",
    )(place, own, before, after, far_lo, far_hi)


def join_sc_kernel(base_ref, a_ref, out_ref):
    out_ref[0] = a_ref[:, 0]


def join_sc(base, full):
    return pl.pallas_call(
        join_sc_kernel,
        grid=(NX,),
        in_specs=[
            pl.BlockSpec(memory_space=pl.ANY),
            pl.BlockSpec((NZ, 1, ROWS_A, COLS), lambda x: (0, x, 0, 0)),
        ],
        out_specs=pl.BlockSpec((1, NZ, ROWS_A, COLS), lambda x: (x, 0, 0, 0)),
        out_shape=jax.ShapeDtypeStruct(FULL, bf16),
        input_output_aliases={0: 0},
        compiler_params=pltpu.CompilerParams(vmem_limit_bytes=60 << 20),
        cost_estimate=pl.CostEstimate(flops=0, bytes_accessed=4 << 20, transcendentals=0),
        name="join_sc",
    )(base, full)


def shift(value, axis, size, by):
    return lax.ppermute(value, axis, [(i, (i + by) % size) for i in range(size)])


def spread(sums, axes, size):
    wide = jnp.broadcast_to(sums[None], (size,) + sums.shape)
    return lax.all_to_all(wide, axes, 0, 0, tiled=True)


def body(x, q, k, v, g, w, m, s):
    x_a, x_b = turn(x[0])
    packed = pack(q[0], k[0], v[0], g[0])
    heads = lax.all_to_all(packed, ("y", "core"), 0, 0, tiled=True).reshape(LENGTH, PACKED)
    x_a = lax.all_gather(x_a, ("y", "core"), axis=0, tiled=False)
    half = NX * NZ // 2
    x_before, x_after = shift(x_b, "y", NY, 1), shift(x_b, "y", NY, -1)
    far_lo = shift(x_before[:half], "y", NY, 1)
    far_hi = shift(x_after[half:], "y", NY, -1)
    pieces = []
    for piece in (x_b, x_before, x_after, far_lo, far_hi):
        pieces += [piece, shift(piece, "core", NCORE, 1)]
    heads, pieces = lax.optimization_barrier((heads, pieces))
    grouped = attention(heads)

    at_x = lax.axis_index("x")
    at_y, at_core = lax.axis_index("y"), lax.axis_index("core")
    blocks = []
    for by in (0, NY - 1, 1, 2):
        for other in (at_core, 1 - at_core):
            blocks.append(((at_y + by) % NY) * NCORE + other)
    offsets = (jnp.stack(blocks) * ROWS).astype(jnp.int32)
    part_a = project_a(at_x.reshape(1).astype(jnp.int32), grouped, x_a)
    part_b = project_b(offsets, grouped, pieces)
    part_a = lax.psum_scatter(part_a, "z", scatter_dimension=0, tiled=True)[0]
    part_b = lax.all_to_all(part_b, "x", 0, 0, tiled=True)
    part_b = jnp.sum(part_b.astype(f32), axis=0).astype(bf16)
    part_b = lax.all_to_all(part_b, "z", 0, 0, tiled=True)
    part_a = [part_a[0]] + [shift(part_a[by], "x", NX, by) for by in range(1, NX)]

    first_new, second_new, direction, mine_a, mine_b, sums = optimizer(part_a, part_b, w, m, s)
    place = jnp.stack([at_x, (at_x + 3) % NX, (at_x + 1) % NX, (at_x + 2) % NX]).astype(jnp.int32)
    pieces = (
        mine_a,
        shift(mine_a, "x", NX, 1),
        shift(mine_a, "x", NX, -1),
        shift(mine_a, "x", NX, 2),
    )
    gathered_b = lax.all_gather(mine_b, "z", axis=0, tiled=False)
    sums = spread(jnp.sum(spread(sums, ("y", "core"), 8), axis=0), ("x", "z"), 32)
    new_a, new_b = apply_step(place, sums, pieces, gathered_b)
    full_a = lax.all_gather(new_a, "z", axis=0, tiled=False)
    before, after = shift(new_b, "x", NX, 1), shift(new_b, "x", NX, -1)
    far_lo = shift(before[: NZ // 2], "x", NX, 1)
    far_hi = shift(after[NZ // 2 :], "x", NX, -1)
    new_weights = join_x(place, new_b, before, after, far_lo, far_hi)
    new_weights = join_sc(new_weights, full_a)

    total = jnp.sum(sums, axis=0)
    lamb_update = (jnp.sqrt(total[0, 0]) / jnp.sqrt(total[1, 0])) * direction
    return first_new, second_new, lamb_update, new_weights.reshape(WIDTH, COLS)


def solution(mesh):
    fine = Mesh(mesh.devices.reshape(NX, NZ, NY, NCORE), ("x", "z", "y", "core"))
    dp, ctx = ("x", "z"), ("y", "core")
    seq = P(dp, ctx, None)
    mat = P(dp, ctx)
    return jax.shard_map(
        body,
        mesh=fine,
        in_specs=(seq, seq, seq, seq, seq, mat, mat, mat),
        out_specs=(mat, mat, mat, P(None, ctx)),
        check_vma=False,
    )
```

```python
import jax
import jax.numpy as jnp
from jax import lax
from jax.experimental import pallas as pl
from jax.experimental.pallas import tpu as pltpu
from jax.sharding import Mesh
from jax.sharding import PartitionSpec as P

HEAD_DIM = 128
STEP = 100
GROUP = 4
NX, NZ, NY, NCORE = 4, 8, 4, 2
LENGTH = 1024
COLS = 768
WIDTH = 4096
ROWS = 128
PACKED = 1280
BLOCK = 256
PART_A = 80
PART_B = ROWS - PART_A
ROWS_A = 64
ROWS_B = ROWS - ROWS_A

beta_first = 0.9
beta_second = 0.999
adam_epsilon = 1e-06
decay_rate = 0.01
learn_rate = 0.01
masked_score = -1e30
score_scale = HEAD_DIM ** (-0.5)
LOG2E = 1.4426950408889634

f32 = jnp.float32
bf16 = jnp.bfloat16


def dot(a, b, ca, cb):
    return lax.dot_general(a, b, (((ca,), (cb,)), ((), ())), preferred_element_type=f32)


def pack_kernel(q_ref, k_ref, v_ref, g_ref, out_ref):
    for c in range(out_ref.shape[0]):
        out_ref[c, :, 0:512] = q_ref[:, c * 512 : (c + 1) * 512]
        out_ref[c, :, 512:640] = k_ref[:, c * 128 : (c + 1) * 128]
        out_ref[c, :, 640:768] = v_ref[:, c * 128 : (c + 1) * 128]
        out_ref[c, :, 768:1280] = g_ref[:, c * 512 : (c + 1) * 512]


def pack(q, k, v, g):
    rows = q.shape[0]
    each = 4
    return pl.pallas_call(
        pack_kernel,
        grid=(8 // each,),
        in_specs=[
            pl.BlockSpec((rows, 512 * each), lambda c: (0, c)),
            pl.BlockSpec((rows, 128 * each), lambda c: (0, c)),
            pl.BlockSpec((rows, 128 * each), lambda c: (0, c)),
            pl.BlockSpec((rows, 512 * each), lambda c: (0, c)),
        ],
        out_specs=pl.BlockSpec((each, rows, PACKED), lambda c: (c, 0, 0)),
        out_shape=jax.ShapeDtypeStruct((8, rows, PACKED), bf16),
        cost_estimate=pl.CostEstimate(flops=0, bytes_accessed=5 << 20, transcendentals=0),
        name="pack",
    )(q, k, v, g)


def turn_kernel(x_ref, out_ref):
    for i in range(out_ref.shape[0]):
        out_ref[i] = x_ref[:, i * ROWS : (i + 1) * ROWS].T


def turn(x):
    tokens = x.shape[0]
    each = 16
    return pl.pallas_call(
        turn_kernel,
        grid=(NX * NZ // each,),
        in_specs=[pl.BlockSpec((tokens, ROWS * each), lambda i: (0, i))],
        out_specs=pl.BlockSpec((each, ROWS, tokens), lambda i: (i, 0, 0)),
        out_shape=jax.ShapeDtypeStruct((NX * NZ, ROWS, tokens), bf16),
        cost_estimate=pl.CostEstimate(flops=0, bytes_accessed=2 << 20, transcendentals=0),
        name="turn",
    )(x)


def attention_kernel(q_ref, k_ref, v_ref, g_ref, out_ref, kt_ref, dk_acc, dv_acc):
    head = pl.program_id(0)

    @pl.when(head == 0)
    def _():
        kt_ref[...] = k_ref[...].T
        dk_acc[...] = jnp.zeros_like(dk_acc)
        dv_acc[...] = jnp.zeros_like(dv_acc)

    key_pos = lax.broadcasted_iota(jnp.int32, (BLOCK, BLOCK), 0)
    query_pos = lax.broadcasted_iota(jnp.int32, (BLOCK, BLOCK), 1)
    allowed = key_pos <= query_pos
    for i in range(LENGTH // BLOCK):
        lo, hi = i * BLOCK, (i + 1) * BLOCK
        q = q_ref[lo:hi, :]
        g = g_ref[lo:hi, :]
        scores = dot(k_ref[:hi, :], q, 1, 1)
        diag = jnp.where(allowed, scores[lo:hi, :], masked_score)
        scores = diag if i == 0 else jnp.concatenate([scores[:lo, :], diag], axis=0)
        top = jnp.max(scores, axis=0, keepdims=True)
        weights = jnp.exp2((scores - top) * (score_scale * LOG2E))
        probs = weights * (1.0 / jnp.sum(weights, axis=0, keepdims=True))
        probs_b = probs.astype(bf16)
        prob_grad = dot(v_ref[:hi, :], g, 1, 1)
        row_delta = jnp.sum(probs_b.astype(f32) * prob_grad, axis=0, keepdims=True)
        dscore = (probs * (prob_grad - row_delta)).astype(bf16)
        dq_t = dot(kt_ref[:, :hi], dscore, 1, 0) * score_scale
        out_ref[lo:hi, pl.ds(pl.multiple_of(head * 128, 128), 128)] = dq_t.astype(bf16).T
        dk_acc[:hi, :] += dot(dscore, q, 1, 0)
        dv_acc[:hi, :] += dot(probs_b, g, 1, 0)

    @pl.when(head == GROUP - 1)
    def _():
        out_ref[:, 512:640] = (dk_acc[...] * score_scale).astype(bf16)
        out_ref[:, 640:768] = dv_acc[...].astype(bf16)


def attention(packed):
    return pl.pallas_call(
        attention_kernel,
        grid=(GROUP,),
        in_specs=[
            pl.BlockSpec((LENGTH, 128), lambda h: (0, h)),
            pl.BlockSpec((LENGTH, 128), lambda h: (0, 4)),
            pl.BlockSpec((LENGTH, 128), lambda h: (0, 5)),
            pl.BlockSpec((LENGTH, 128), lambda h: (0, 6 + h)),
        ],
        out_specs=pl.BlockSpec((LENGTH, COLS), lambda h: (0, 0)),
        out_shape=jax.ShapeDtypeStruct((LENGTH, COLS), bf16),
        scratch_shapes=[
            pltpu.VMEM((128, LENGTH), bf16),
            pltpu.VMEM((LENGTH, 128), f32),
            pltpu.VMEM((LENGTH, 128), f32),
        ],
        compiler_params=pltpu.CompilerParams(vmem_limit_bytes=48 << 20),
        cost_estimate=pl.CostEstimate(
            flops=4 << 30, bytes_accessed=5 << 20, transcendentals=4 << 20
        ),
        name="attention_backward",
    )(packed, packed, packed, packed)


def project(grouped, x, lo, hi, at_x, name):
    part = hi - lo

    def kernel(place, grouped_ref, x_ref, out_ref):
        rows = jnp.concatenate(
            [x_ref[t, :, lo:hi, :].reshape(NZ * part, ROWS) for t in range(8)], axis=1
        )
        res = dot(rows, grouped_ref[...], 1, 0).astype(bf16)
        out_ref[...] = res.reshape(out_ref.shape)

    if at_x is None:
        shape, block = (NX, NZ, part, COLS), (1, NZ, part, COLS)
        out_map = lambda x, place: (x, 0, 0, 0)
        at_x = jnp.zeros((1,), jnp.int32)
    else:
        shape, block = (NZ, NX, part, COLS), (NZ, 1, part, COLS)
        out_map = lambda x, place: (0, lax.rem(x - place[0] + NX, NX), 0, 0)
    return pl.pallas_call(
        kernel,
        grid_spec=pltpu.PrefetchScalarGridSpec(
            num_scalar_prefetch=1,
            grid=(NX,),
            in_specs=[
                pl.BlockSpec((LENGTH, COLS), lambda x, place: (0, 0)),
                pl.BlockSpec((8, NZ, ROWS, ROWS), lambda x, place: (0, x, 0, 0)),
            ],
            out_specs=pl.BlockSpec(block, out_map),
        ),
        out_shape=jax.ShapeDtypeStruct(shape, bf16),
        compiler_params=pltpu.CompilerParams(vmem_limit_bytes=60 << 20),
        cost_estimate=pl.CostEstimate(
            flops=2 * LENGTH * COLS * WIDTH * part // ROWS,
            bytes_accessed=12 << 20,
            transcendentals=0,
        ),
        name=name,
    )(at_x, grouped, x)


def optimizer_kernel(ga0, ga1, ga2, ga3, gb_ref, w_ref, m_ref, v_ref, m_out, v_out, dir_out, a_out, b_out, sums_out):
    grad_a = ga0[...].astype(f32) + ga1[...].astype(f32)
    grad_a = grad_a + ga2[...].astype(f32) + ga3[...].astype(f32)
    grad_b = jnp.sum(gb_ref[...].astype(f32), axis=0)
    gradient = jnp.concatenate([grad_a, grad_b], axis=0)
    weight = w_ref[...]
    first_new = beta_first * m_ref[...] + (1.0 - beta_first) * gradient
    second_new = beta_second * v_ref[...] + (1.0 - beta_second) * gradient * gradient
    corr_first = 1.0 - beta_first**STEP
    corr_second = 1.0 - beta_second**STEP
    direction = (
        first_new / corr_first / (jnp.sqrt(second_new / corr_second) + adam_epsilon)
        + decay_rate * weight
    )
    m_out[...] = first_new
    v_out[...] = second_new
    dir_out[...] = direction
    a_out[0] = direction[:ROWS_A].astype(bf16)
    a_out[1] = weight[:ROWS_A].astype(bf16)
    b_out[0] = direction[ROWS_A:].astype(bf16)
    b_out[1] = weight[ROWS_A:].astype(bf16)
    weight_sq = jnp.sum(weight * weight)
    update_sq = jnp.sum(direction * direction)
    row = lax.broadcasted_iota(jnp.int32, (8, 128), 0)
    sums_out[...] = jnp.where(row == 0, weight_sq, update_sq)


def optimizer(ga, gb, w, m, v):
    shape = jax.ShapeDtypeStruct((ROWS, COLS), f32)
    return pl.pallas_call(
        optimizer_kernel,
        out_shape=[
            shape,
            shape,
            shape,
            jax.ShapeDtypeStruct((2, ROWS_A, COLS), bf16),
            jax.ShapeDtypeStruct((2, ROWS_B, COLS), bf16),
            jax.ShapeDtypeStruct((8, 128), f32),
        ],
        compiler_params=pltpu.CompilerParams(vmem_limit_bytes=32 << 20),
        name="optimizer",
    )(*ga, gb, w, m, v)


def apply_kernel(place_ref, sums_ref, a0, a1, a2, a3, b_ref, a_out, b_out):
    sums = jnp.sum(sums_ref[...], axis=0)
    rate = learn_rate * (jnp.sqrt(sums[0:1, 0:1]) / jnp.sqrt(sums[1:2, 0:1]))
    for k, ref in enumerate((a0, a1, a2, a3)):
        new = ref[1].astype(f32) - rate * ref[0].astype(f32)
        a_out[place_ref[k]] = new.astype(bf16)
    for z in range(NZ):
        new = b_ref[z, 1].astype(f32) - rate * b_ref[z, 0].astype(f32)
        b_out[z] = new.astype(bf16)


def apply_step(place, sums, pieces, gathered):
    vmem = pl.BlockSpec(memory_space=pltpu.VMEM)
    return pl.pallas_call(
        apply_kernel,
        in_specs=[pl.BlockSpec(memory_space=pltpu.SMEM)] + [vmem] * 6,
        out_specs=[vmem, vmem],
        out_shape=[
            jax.ShapeDtypeStruct((NX, ROWS_A, COLS), bf16),
            jax.ShapeDtypeStruct((NZ, ROWS_B, COLS), bf16),
        ],
        compiler_params=pltpu.CompilerParams(vmem_limit_bytes=32 << 20),
        name="apply",
    )(place, sums, *pieces, gathered)


FULL = (NX, NZ, ROWS, COLS)


def join_x_kernel(place_ref, b0, b1, b2, b3, b4, out_ref):
    step, half = pl.program_id(0), pl.program_id(1)
    for k, ref in enumerate((b0, b1, b2)):

        @pl.when(step == k)
        def _(ref=ref):
            out_ref[0] = ref[...]

    for k, ref in enumerate((b3, b4)):

        @pl.when((step == 3) & (half == k))
        def _(ref=ref):
            out_ref[0] = ref[...]


def join_x(place, own, before, after, far_lo, far_hi):
    half = NZ // 2

    def b_spec(k):
        return pl.BlockSpec(
            (half, ROWS_B, COLS),
            lambda o, h, place: (jnp.where(o < k, 0, jnp.where(o > k, 1, h)), 0, 0),
        )

    whole = pl.BlockSpec((half, ROWS_B, COLS), lambda o, h, place: (0, 0, 0))
    return pl.pallas_call(
        join_x_kernel,
        grid_spec=pltpu.PrefetchScalarGridSpec(
            num_scalar_prefetch=1,
            grid=(NX, 2),
            in_specs=[b_spec(0), b_spec(1), b_spec(2), whole, whole],
            out_specs=pl.BlockSpec(
                (1, half, ROWS_B, COLS),
                lambda o, h, place: (place[o], h, ROWS_A // ROWS_B, 0),
            ),
        ),
        out_shape=jax.ShapeDtypeStruct(FULL, bf16),
        compiler_params=pltpu.CompilerParams(vmem_limit_bytes=48 << 20),
        cost_estimate=pl.CostEstimate(flops=0, bytes_accessed=7 << 20, transcendentals=0),
        name="join_x",
    )(place, own, before, after, far_lo, far_hi)


def join_sc_kernel(base_ref, a_ref, out_ref):
    out_ref[0] = a_ref[:, 0]


def join_sc(base, full):
    return pl.pallas_call(
        join_sc_kernel,
        grid=(NX,),
        in_specs=[
            pl.BlockSpec(memory_space=pl.ANY),
            pl.BlockSpec((NZ, 1, ROWS_A, COLS), lambda x: (0, x, 0, 0)),
        ],
        out_specs=pl.BlockSpec((1, NZ, ROWS_A, COLS), lambda x: (x, 0, 0, 0)),
        out_shape=jax.ShapeDtypeStruct(FULL, bf16),
        input_output_aliases={0: 0},
        compiler_params=pltpu.CompilerParams(vmem_limit_bytes=60 << 20),
        cost_estimate=pl.CostEstimate(flops=0, bytes_accessed=4 << 20, transcendentals=0),
        name="join_sc",
    )(base, full)


def shift(value, axis, size, by):
    return lax.ppermute(value, axis, [(i, (i + by) % size) for i in range(size)])


def spread(sums, axes, size):
    wide = jnp.broadcast_to(sums[None], (size,) + sums.shape)
    return lax.all_to_all(wide, axes, 0, 0, tiled=True)


def body(x, q, k, v, g, w, m, s):
    x_turned = turn(x[0])
    packed = pack(q[0], k[0], v[0], g[0])
    heads = lax.all_to_all(packed, ("y", "core"), 0, 0, tiled=True).reshape(LENGTH, PACKED)
    x_full = lax.all_gather(x_turned, ("y", "core"), axis=0, tiled=False)
    grouped = attention(heads)

    at_x = lax.axis_index("x")
    place_x = at_x.reshape(1).astype(jnp.int32)
    part_a = project(grouped, x_full, 0, PART_A, place_x, "project_a")
    part_b = project(grouped, x_full, PART_A, ROWS, None, "project_b")
    part_a = lax.psum_scatter(part_a, "z", scatter_dimension=0, tiled=True)[0]
    part_b = lax.all_to_all(part_b, "x", 0, 0, tiled=True)
    part_b = jnp.sum(part_b.astype(f32), axis=0).astype(bf16)
    part_b = lax.all_to_all(part_b, "z", 0, 0, tiled=True)
    part_a = [part_a[0]] + [shift(part_a[by], "x", NX, by) for by in range(1, NX)]

    first_new, second_new, direction, mine_a, mine_b, sums = optimizer(part_a, part_b, w, m, s)
    place = jnp.stack([at_x, (at_x + 3) % NX, (at_x + 1) % NX, (at_x + 2) % NX]).astype(jnp.int32)
    pieces = (
        mine_a,
        shift(mine_a, "x", NX, 1),
        shift(mine_a, "x", NX, -1),
        shift(mine_a, "x", NX, 2),
    )
    gathered_b = lax.all_gather(mine_b, "z", axis=0, tiled=False)
    sums = spread(jnp.sum(spread(sums, ("y", "core"), 8), axis=0), ("x", "z"), 32)
    new_a, new_b = apply_step(place, sums, pieces, gathered_b)
    full_a = lax.all_gather(new_a, "z", axis=0, tiled=False)
    before, after = shift(new_b, "x", NX, 1), shift(new_b, "x", NX, -1)
    far_lo = shift(before[: NZ // 2], "x", NX, 1)
    far_hi = shift(after[NZ // 2 :], "x", NX, -1)
    new_weights = join_x(place, new_b, before, after, far_lo, far_hi)
    new_weights = join_sc(new_weights, full_a)

    total = jnp.sum(sums, axis=0)
    lamb_update = (jnp.sqrt(total[0, 0]) / jnp.sqrt(total[1, 0])) * direction
    return first_new, second_new, lamb_update, new_weights.reshape(WIDTH, COLS)


def solution(mesh):
    fine = Mesh(mesh.devices.reshape(NX, NZ, NY, NCORE), ("x", "z", "y", "core"))
    dp, ctx = ("x", "z"), ("y", "core")
    seq = P(dp, ctx, None)
    mat = P(dp, ctx)
    return jax.shard_map(
        body,
        mesh=fine,
        in_specs=(seq, seq, seq, seq, seq, mat, mat, mat),
        out_specs=(mat, mat, mat, P(None, ctx)),
        check_vma=False,
    )
```

```python
import jax
import jax.numpy as jnp
from jax import lax
from jax.experimental import pallas as pl
from jax.experimental.pallas import tpu as pltpu
from jax.sharding import Mesh
from jax.sharding import PartitionSpec as P

HEAD_DIM = 128
STEP = 100
GROUP = 4
NX, NZ, NY, NCORE = 4, 8, 4, 2
LENGTH = 1024
COLS = 768
WIDTH = 4096
ROWS = 128
PACKED = 1280
BLOCK = 256
PART_A = 80
PART_B = ROWS - PART_A
ROWS_A = 64
ROWS_B = ROWS - ROWS_A

beta_first = 0.9
beta_second = 0.999
adam_epsilon = 1e-06
decay_rate = 0.01
learn_rate = 0.01
masked_score = -1e30
score_scale = HEAD_DIM ** (-0.5)
LOG2E = 1.4426950408889634

f32 = jnp.float32
bf16 = jnp.bfloat16


def dot(a, b, ca, cb):
    return lax.dot_general(a, b, (((ca,), (cb,)), ((), ())), preferred_element_type=f32)


def pack_kernel(q_ref, k_ref, v_ref, g_ref, out_ref):
    for c in range(out_ref.shape[0]):
        out_ref[c, :, 0:512] = q_ref[:, c * 512 : (c + 1) * 512]
        out_ref[c, :, 512:640] = k_ref[:, c * 128 : (c + 1) * 128]
        out_ref[c, :, 640:768] = v_ref[:, c * 128 : (c + 1) * 128]
        out_ref[c, :, 768:1280] = g_ref[:, c * 512 : (c + 1) * 512]


def pack(q, k, v, g):
    rows = q.shape[0]
    each = 4
    return pl.pallas_call(
        pack_kernel,
        grid=(8 // each,),
        in_specs=[
            pl.BlockSpec((rows, 512 * each), lambda c: (0, c)),
            pl.BlockSpec((rows, 128 * each), lambda c: (0, c)),
            pl.BlockSpec((rows, 128 * each), lambda c: (0, c)),
            pl.BlockSpec((rows, 512 * each), lambda c: (0, c)),
        ],
        out_specs=pl.BlockSpec((each, rows, PACKED), lambda c: (c, 0, 0)),
        out_shape=jax.ShapeDtypeStruct((8, rows, PACKED), bf16),
        cost_estimate=pl.CostEstimate(flops=0, bytes_accessed=5 << 20, transcendentals=0),
        name="pack",
    )(q, k, v, g)


def turn_kernel(x_ref, out_ref):
    for i in range(out_ref.shape[0]):
        out_ref[i] = x_ref[:, i * ROWS : (i + 1) * ROWS].T


def turn(x):
    tokens = x.shape[0]
    each = 16
    return pl.pallas_call(
        turn_kernel,
        grid=(NX * NZ // each,),
        in_specs=[pl.BlockSpec((tokens, ROWS * each), lambda i: (0, i))],
        out_specs=pl.BlockSpec((each, ROWS, tokens), lambda i: (i, 0, 0)),
        out_shape=jax.ShapeDtypeStruct((NX * NZ, ROWS, tokens), bf16),
        cost_estimate=pl.CostEstimate(flops=0, bytes_accessed=2 << 20, transcendentals=0),
        name="turn",
    )(x)


def attention_kernel(q_ref, k_ref, v_ref, g_ref, out_ref, kt_ref, dk_acc, dv_acc):
    head = pl.program_id(0)

    @pl.when(head == 0)
    def _():
        kt_ref[...] = k_ref[...].T
        dk_acc[...] = jnp.zeros_like(dk_acc)
        dv_acc[...] = jnp.zeros_like(dv_acc)

    key_pos = lax.broadcasted_iota(jnp.int32, (BLOCK, BLOCK), 0)
    query_pos = lax.broadcasted_iota(jnp.int32, (BLOCK, BLOCK), 1)
    allowed = key_pos <= query_pos
    for i in range(LENGTH // BLOCK):
        lo, hi = i * BLOCK, (i + 1) * BLOCK
        q = q_ref[lo:hi, :]
        g = g_ref[lo:hi, :]
        scores = dot(k_ref[:hi, :], q, 1, 1)
        diag = jnp.where(allowed, scores[lo:hi, :], masked_score)
        scores = diag if i == 0 else jnp.concatenate([scores[:lo, :], diag], axis=0)
        top = jnp.max(scores, axis=0, keepdims=True)
        weights = jnp.exp2((scores - top) * (score_scale * LOG2E))
        probs = weights * (1.0 / jnp.sum(weights, axis=0, keepdims=True))
        probs_b = probs.astype(bf16)
        prob_grad = dot(v_ref[:hi, :], g, 1, 1)
        row_delta = jnp.sum(probs_b.astype(f32) * prob_grad, axis=0, keepdims=True)
        dscore = (probs * (prob_grad - row_delta)).astype(bf16)
        dq_t = dot(kt_ref[:, :hi], dscore, 1, 0) * score_scale
        out_ref[lo:hi, pl.ds(pl.multiple_of(head * 128, 128), 128)] = dq_t.astype(bf16).T
        dk_acc[:hi, :] += dot(dscore, q, 1, 0)
        dv_acc[:hi, :] += dot(probs_b, g, 1, 0)

    @pl.when(head == GROUP - 1)
    def _():
        out_ref[:, 512:640] = (dk_acc[...] * score_scale).astype(bf16)
        out_ref[:, 640:768] = dv_acc[...].astype(bf16)


def attention(packed):
    return pl.pallas_call(
        attention_kernel,
        grid=(GROUP,),
        in_specs=[
            pl.BlockSpec((LENGTH, 128), lambda h: (0, h)),
            pl.BlockSpec((LENGTH, 128), lambda h: (0, 4)),
            pl.BlockSpec((LENGTH, 128), lambda h: (0, 5)),
            pl.BlockSpec((LENGTH, 128), lambda h: (0, 6 + h)),
        ],
        out_specs=pl.BlockSpec((LENGTH, COLS), lambda h: (0, 0)),
        out_shape=jax.ShapeDtypeStruct((LENGTH, COLS), bf16),
        scratch_shapes=[
            pltpu.VMEM((128, LENGTH), bf16),
            pltpu.VMEM((LENGTH, 128), f32),
            pltpu.VMEM((LENGTH, 128), f32),
        ],
        compiler_params=pltpu.CompilerParams(vmem_limit_bytes=62 << 20),
        cost_estimate=pl.CostEstimate(
            flops=4 << 30, bytes_accessed=5 << 20, transcendentals=4 << 20
        ),
        name="attention_backward",
    )(packed, packed, packed, packed)


def project_kernel(place, grouped_ref, x_ref, a_ref, b_ref):
    rows = jnp.concatenate([x_ref[t].reshape(NZ * ROWS, ROWS) for t in range(8)], axis=1)
    res = dot(rows, grouped_ref[...], 1, 0).astype(bf16).reshape(NZ, ROWS, COLS)
    a_ref[:, 0] = res[:, :PART_A]
    b_ref[0] = res[:, PART_A:]


def project(at_x, grouped, x):
    return pl.pallas_call(
        project_kernel,
        grid_spec=pltpu.PrefetchScalarGridSpec(
            num_scalar_prefetch=1,
            grid=(NX,),
            in_specs=[
                pl.BlockSpec((LENGTH, COLS), lambda x, place: (0, 0)),
                pl.BlockSpec((8, NZ, ROWS, ROWS), lambda x, place: (0, x, 0, 0)),
            ],
            out_specs=[
                pl.BlockSpec(
                    (NZ, 1, PART_A, COLS),
                    lambda x, place: (0, lax.rem(x - place[0] + NX, NX), 0, 0),
                ),
                pl.BlockSpec((1, NZ, PART_B, COLS), lambda x, place: (x, 0, 0, 0)),
            ],
        ),
        out_shape=[
            jax.ShapeDtypeStruct((NZ, NX, PART_A, COLS), bf16),
            jax.ShapeDtypeStruct((NX, NZ, PART_B, COLS), bf16),
        ],
        compiler_params=pltpu.CompilerParams(vmem_limit_bytes=62 << 20),
        cost_estimate=pl.CostEstimate(flops=6 << 30, bytes_accessed=16 << 20, transcendentals=0),
        name="project",
    )(at_x, grouped, x)


def fold_kernel(part_ref, out_ref):
    out_ref[...] = jnp.sum(part_ref[...].astype(f32), axis=0).astype(bf16)


def fold(part):
    return pl.pallas_call(
        fold_kernel,
        grid=(4,),
        in_specs=[pl.BlockSpec((NX, NZ // 4, PART_B, COLS), lambda z: (0, z, 0, 0))],
        out_specs=pl.BlockSpec((NZ // 4, PART_B, COLS), lambda z: (z, 0, 0)),
        out_shape=jax.ShapeDtypeStruct((NZ, PART_B, COLS), bf16),
        compiler_params=pltpu.CompilerParams(vmem_limit_bytes=60 << 20),
        cost_estimate=pl.CostEstimate(flops=0, bytes_accessed=3 << 20, transcendentals=0),
        name="fold",
    )(part)


def optimizer_kernel(ga0, ga1, ga2, ga3, gb_ref, w_ref, m_ref, v_ref, m_out, v_out, dir_out, a_out, b_out, sums_out):
    grad_a = ga0[...].astype(f32) + ga1[...].astype(f32)
    grad_a = grad_a + ga2[...].astype(f32) + ga3[...].astype(f32)
    grad_b = jnp.sum(gb_ref[...].astype(f32), axis=0)
    gradient = jnp.concatenate([grad_a, grad_b], axis=0)
    weight = w_ref[...]
    first_new = beta_first * m_ref[...] + (1.0 - beta_first) * gradient
    second_new = beta_second * v_ref[...] + (1.0 - beta_second) * gradient * gradient
    corr_first = 1.0 - beta_first**STEP
    corr_second = 1.0 - beta_second**STEP
    direction = (
        first_new / corr_first / (jnp.sqrt(second_new / corr_second) + adam_epsilon)
        + decay_rate * weight
    )
    m_out[...] = first_new
    v_out[...] = second_new
    dir_out[...] = direction
    a_out[0] = direction[:ROWS_A].astype(bf16)
    a_out[1] = weight[:ROWS_A].astype(bf16)
    b_out[0] = direction[ROWS_A:].astype(bf16)
    b_out[1] = weight[ROWS_A:].astype(bf16)
    weight_sq = jnp.sum(weight * weight)
    update_sq = jnp.sum(direction * direction)
    row = lax.broadcasted_iota(jnp.int32, (8, 128), 0)
    sums_out[...] = jnp.where(row == 0, weight_sq, update_sq)


def optimizer(ga, gb, w, m, v):
    shape = jax.ShapeDtypeStruct((ROWS, COLS), f32)
    return pl.pallas_call(
        optimizer_kernel,
        out_shape=[
            shape,
            shape,
            shape,
            jax.ShapeDtypeStruct((2, ROWS_A, COLS), bf16),
            jax.ShapeDtypeStruct((2, ROWS_B, COLS), bf16),
            jax.ShapeDtypeStruct((8, 128), f32),
        ],
        compiler_params=pltpu.CompilerParams(vmem_limit_bytes=32 << 20),
        name="optimizer",
    )(*ga, gb, w, m, v)


def apply_kernel(place_ref, sums_ref, a0, a1, a2, a3, b_ref, a_out, b_out):
    sums = jnp.sum(sums_ref[...], axis=0)
    rate = learn_rate * (jnp.sqrt(sums[0:1, 0:1]) / jnp.sqrt(sums[1:2, 0:1]))
    for k, ref in enumerate((a0, a1, a2, a3)):
        new = ref[1].astype(f32) - rate * ref[0].astype(f32)
        a_out[place_ref[k]] = new.astype(bf16)
    for z in range(NZ):
        new = b_ref[z, 1].astype(f32) - rate * b_ref[z, 0].astype(f32)
        b_out[z] = new.astype(bf16)


def apply_step(place, sums, pieces, gathered):
    vmem = pl.BlockSpec(memory_space=pltpu.VMEM)
    return pl.pallas_call(
        apply_kernel,
        in_specs=[pl.BlockSpec(memory_space=pltpu.SMEM)] + [vmem] * 6,
        out_specs=[vmem, vmem],
        out_shape=[
            jax.ShapeDtypeStruct((NX, ROWS_A, COLS), bf16),
            jax.ShapeDtypeStruct((NZ, ROWS_B, COLS), bf16),
        ],
        compiler_params=pltpu.CompilerParams(vmem_limit_bytes=32 << 20),
        name="apply",
    )(place, sums, *pieces, gathered)


FULL = (NX, NZ, ROWS, COLS)


def join_x_kernel(place_ref, b0, b1, b2, b3, b4, out_ref):
    step, half = pl.program_id(0), pl.program_id(1)
    for k, ref in enumerate((b0, b1, b2)):

        @pl.when(step == k)
        def _(ref=ref):
            out_ref[0] = ref[...]

    for k, ref in enumerate((b3, b4)):

        @pl.when((step == 3) & (half == k))
        def _(ref=ref):
            out_ref[0] = ref[...]


def join_x(place, own, before, after, far_lo, far_hi):
    half = NZ // 2

    def b_spec(k):
        return pl.BlockSpec(
            (half, ROWS_B, COLS),
            lambda o, h, place: (jnp.where(o < k, 0, jnp.where(o > k, 1, h)), 0, 0),
        )

    whole = pl.BlockSpec((half, ROWS_B, COLS), lambda o, h, place: (0, 0, 0))
    return pl.pallas_call(
        join_x_kernel,
        grid_spec=pltpu.PrefetchScalarGridSpec(
            num_scalar_prefetch=1,
            grid=(NX, 2),
            in_specs=[b_spec(0), b_spec(1), b_spec(2), whole, whole],
            out_specs=pl.BlockSpec(
                (1, half, ROWS_B, COLS),
                lambda o, h, place: (place[o], h, ROWS_A // ROWS_B, 0),
            ),
        ),
        out_shape=jax.ShapeDtypeStruct(FULL, bf16),
        compiler_params=pltpu.CompilerParams(vmem_limit_bytes=48 << 20),
        cost_estimate=pl.CostEstimate(flops=0, bytes_accessed=7 << 20, transcendentals=0),
        name="join_x",
    )(place, own, before, after, far_lo, far_hi)


def join_sc_kernel(base_ref, a_ref, out_ref):
    out_ref[0] = a_ref[:, 0]


def join_sc(base, full):
    return pl.pallas_call(
        join_sc_kernel,
        grid=(NX,),
        in_specs=[
            pl.BlockSpec(memory_space=pl.ANY),
            pl.BlockSpec((NZ, 1, ROWS_A, COLS), lambda x: (0, x, 0, 0)),
        ],
        out_specs=pl.BlockSpec((1, NZ, ROWS_A, COLS), lambda x: (x, 0, 0, 0)),
        out_shape=jax.ShapeDtypeStruct(FULL, bf16),
        input_output_aliases={0: 0},
        compiler_params=pltpu.CompilerParams(vmem_limit_bytes=60 << 20),
        cost_estimate=pl.CostEstimate(flops=0, bytes_accessed=4 << 20, transcendentals=0),
        name="join_sc",
    )(base, full)


def shift(value, axis, size, by):
    return lax.ppermute(value, axis, [(i, (i + by) % size) for i in range(size)])


def spread(sums, axes, size):
    wide = jnp.broadcast_to(sums[None], (size,) + sums.shape)
    return lax.all_to_all(wide, axes, 0, 0, tiled=True)


def body(x, q, k, v, g, w, m, s):
    x_turned = turn(x[0])
    packed = pack(q[0], k[0], v[0], g[0])
    heads = lax.all_to_all(packed, ("y", "core"), 0, 0, tiled=True).reshape(LENGTH, PACKED)
    x_full = lax.all_gather(x_turned, ("y", "core"), axis=0, tiled=False)
    grouped = attention(heads)

    at_x = lax.axis_index("x")
    place_x = at_x.reshape(1).astype(jnp.int32)
    part_a, part_b = project(place_x, grouped, x_full)
    part_a = lax.psum_scatter(part_a, "z", scatter_dimension=0, tiled=True)[0]
    part_b = lax.all_to_all(part_b, "x", 0, 0, tiled=True)
    part_b = fold(part_b)
    part_b = lax.all_to_all(part_b, "z", 0, 0, tiled=True)
    part_a = [part_a[0]] + [shift(part_a[by], "x", NX, by) for by in range(1, NX)]

    first_new, second_new, direction, mine_a, mine_b, sums = optimizer(part_a, part_b, w, m, s)
    place = jnp.stack([at_x, (at_x + 3) % NX, (at_x + 1) % NX, (at_x + 2) % NX]).astype(jnp.int32)
    pieces = (
        mine_a,
        shift(mine_a, "x", NX, 1),
        shift(mine_a, "x", NX, -1),
        shift(mine_a, "x", NX, 2),
    )
    gathered_b = lax.all_gather(mine_b, "z", axis=0, tiled=False)
    sums = spread(jnp.sum(spread(sums, ("y", "core"), 8), axis=0), ("x", "z"), 32)
    new_a, new_b = apply_step(place, sums, pieces, gathered_b)
    full_a = lax.all_gather(new_a, "z", axis=0, tiled=False)
    before, after = shift(new_b, "x", NX, 1), shift(new_b, "x", NX, -1)
    far_lo = shift(before[: NZ // 2], "x", NX, 1)
    far_hi = shift(after[NZ // 2 :], "x", NX, -1)
    new_weights = join_x(place, new_b, before, after, far_lo, far_hi)
    new_weights = join_sc(new_weights, full_a)

    total = jnp.sum(sums, axis=0)
    lamb_update = (jnp.sqrt(total[0, 0]) / jnp.sqrt(total[1, 0])) * direction
    return first_new, second_new, lamb_update, new_weights.reshape(WIDTH, COLS)


def solution(mesh):
    fine = Mesh(mesh.devices.reshape(NX, NZ, NY, NCORE), ("x", "z", "y", "core"))
    dp, ctx = ("x", "z"), ("y", "core")
    seq = P(dp, ctx, None)
    mat = P(dp, ctx)
    return jax.shard_map(
        body,
        mesh=fine,
        in_specs=(seq, seq, seq, seq, seq, mat, mat, mat),
        out_specs=(mat, mat, mat, P(None, ctx)),
        check_vma=False,
    )
```

```python
import jax
import jax.numpy as jnp
from jax import lax
from jax.experimental import pallas as pl
from jax.experimental.pallas import tpu as pltpu
from jax.sharding import Mesh
from jax.sharding import PartitionSpec as P

HEAD_DIM = 128
STEP = 100
GROUP = 4
NX, NZ, NY, NCORE = 4, 8, 4, 2
LENGTH = 1024
COLS = 768
WIDTH = 4096
ROWS = 128
PACKED = 1280
BLOCK = 256
PART_A = 80
PART_B = ROWS - PART_A
ROWS_A = 64
ROWS_B = ROWS - ROWS_A

beta_first = 0.9
beta_second = 0.999
adam_epsilon = 1e-06
decay_rate = 0.01
learn_rate = 0.01
masked_score = -1e30
score_scale = HEAD_DIM ** (-0.5)
LOG2E = 1.4426950408889634

f32 = jnp.float32
bf16 = jnp.bfloat16


def dot(a, b, ca, cb):
    return lax.dot_general(a, b, (((ca,), (cb,)), ((), ())), preferred_element_type=f32)


def pack_kernel(q_ref, k_ref, v_ref, g_ref, out_ref):
    for c in range(out_ref.shape[0]):
        out_ref[c, :, 0:512] = q_ref[:, c * 512 : (c + 1) * 512]
        out_ref[c, :, 512:640] = k_ref[:, c * 128 : (c + 1) * 128]
        out_ref[c, :, 640:768] = v_ref[:, c * 128 : (c + 1) * 128]
        out_ref[c, :, 768:1280] = g_ref[:, c * 512 : (c + 1) * 512]


def pack(q, k, v, g):
    rows = q.shape[0]
    each = 4
    return pl.pallas_call(
        pack_kernel,
        grid=(8 // each,),
        in_specs=[
            pl.BlockSpec((rows, 512 * each), lambda c: (0, c)),
            pl.BlockSpec((rows, 128 * each), lambda c: (0, c)),
            pl.BlockSpec((rows, 128 * each), lambda c: (0, c)),
            pl.BlockSpec((rows, 512 * each), lambda c: (0, c)),
        ],
        out_specs=pl.BlockSpec((each, rows, PACKED), lambda c: (c, 0, 0)),
        out_shape=jax.ShapeDtypeStruct((8, rows, PACKED), bf16),
        cost_estimate=pl.CostEstimate(flops=0, bytes_accessed=5 << 20, transcendentals=0),
        name="pack",
    )(q, k, v, g)


def turn_kernel(x_ref, out_ref):
    for i in range(out_ref.shape[0]):
        out_ref[i] = x_ref[:, i * ROWS : (i + 1) * ROWS].T


def turn(x):
    tokens = x.shape[0]
    each = 16
    return pl.pallas_call(
        turn_kernel,
        grid=(NX * NZ // each,),
        in_specs=[pl.BlockSpec((tokens, ROWS * each), lambda i: (0, i))],
        out_specs=pl.BlockSpec((each, ROWS, tokens), lambda i: (i, 0, 0)),
        out_shape=jax.ShapeDtypeStruct((NX * NZ, ROWS, tokens), bf16),
        cost_estimate=pl.CostEstimate(flops=0, bytes_accessed=2 << 20, transcendentals=0),
        name="turn",
    )(x)


def attention_kernel(q_ref, k_ref, v_ref, g_ref, out_ref, kt_ref, dk_acc, dv_acc):
    head = pl.program_id(0)

    @pl.when(head == 0)
    def _():
        kt_ref[...] = k_ref[...].T
        dk_acc[...] = jnp.zeros_like(dk_acc)
        dv_acc[...] = jnp.zeros_like(dv_acc)

    key_pos = lax.broadcasted_iota(jnp.int32, (BLOCK, BLOCK), 0)
    query_pos = lax.broadcasted_iota(jnp.int32, (BLOCK, BLOCK), 1)
    allowed = key_pos <= query_pos
    for i in range(LENGTH // BLOCK):
        lo, hi = i * BLOCK, (i + 1) * BLOCK
        q = q_ref[lo:hi, :]
        g = g_ref[lo:hi, :]
        scores = dot(k_ref[:hi, :], q, 1, 1)
        diag = jnp.where(allowed, scores[lo:hi, :], masked_score)
        scores = diag if i == 0 else jnp.concatenate([scores[:lo, :], diag], axis=0)
        top = jnp.max(scores, axis=0, keepdims=True)
        weights = jnp.exp2((scores - top) * (score_scale * LOG2E))
        probs = weights * (1.0 / jnp.sum(weights, axis=0, keepdims=True))
        probs_b = probs.astype(bf16)
        prob_grad = dot(v_ref[:hi, :], g, 1, 1)
        row_delta = jnp.sum(probs_b.astype(f32) * prob_grad, axis=0, keepdims=True)
        dscore = (probs * (prob_grad - row_delta)).astype(bf16)
        dq_t = dot(kt_ref[:, :hi], dscore, 1, 0) * score_scale
        out_ref[lo:hi, pl.ds(pl.multiple_of(head * 128, 128), 128)] = dq_t.astype(bf16).T
        dk_acc[:hi, :] += dot(dscore, q, 1, 0)
        dv_acc[:hi, :] += dot(probs_b, g, 1, 0)

    @pl.when(head == GROUP - 1)
    def _():
        out_ref[:, 512:640] = (dk_acc[...] * score_scale).astype(bf16)
        out_ref[:, 640:768] = dv_acc[...].astype(bf16)


def attention(packed):
    return pl.pallas_call(
        attention_kernel,
        grid=(GROUP,),
        in_specs=[
            pl.BlockSpec((LENGTH, 128), lambda h: (0, h)),
            pl.BlockSpec((LENGTH, 128), lambda h: (0, 4)),
            pl.BlockSpec((LENGTH, 128), lambda h: (0, 5)),
            pl.BlockSpec((LENGTH, 128), lambda h: (0, 6 + h)),
        ],
        out_specs=pl.BlockSpec((LENGTH, COLS), lambda h: (0, 0)),
        out_shape=jax.ShapeDtypeStruct((LENGTH, COLS), bf16),
        scratch_shapes=[
            pltpu.VMEM((128, LENGTH), bf16),
            pltpu.VMEM((LENGTH, 128), f32),
            pltpu.VMEM((LENGTH, 128), f32),
        ],
        compiler_params=pltpu.CompilerParams(vmem_limit_bytes=48 << 20),
        cost_estimate=pl.CostEstimate(
            flops=4 << 30, bytes_accessed=5 << 20, transcendentals=4 << 20
        ),
        name="attention_backward",
    )(packed, packed, packed, packed)


def project(grouped, x, lo, hi, at_x, name):
    part = hi - lo

    def kernel(place, grouped_ref, x_ref, out_ref):
        rows = jnp.concatenate(
            [x_ref[t, :, lo:hi, :].reshape(NZ * part, ROWS) for t in range(8)], axis=1
        )
        res = dot(rows, grouped_ref[...], 1, 0).astype(bf16)
        out_ref[...] = res.reshape(out_ref.shape)

    if at_x is None:
        shape, block = (NX, NZ, part, COLS), (1, NZ, part, COLS)
        out_map = lambda x, place: (x, 0, 0, 0)
        at_x = jnp.zeros((1,), jnp.int32)
    else:
        shape, block = (NZ, NX, part, COLS), (NZ, 1, part, COLS)
        out_map = lambda x, place: (0, lax.rem(x - place[0] + NX, NX), 0, 0)
    return pl.pallas_call(
        kernel,
        grid_spec=pltpu.PrefetchScalarGridSpec(
            num_scalar_prefetch=1,
            grid=(NX,),
            in_specs=[
                pl.BlockSpec((LENGTH, COLS), lambda x, place: (0, 0)),
                pl.BlockSpec((8, NZ, ROWS, ROWS), lambda x, place: (0, x, 0, 0)),
            ],
            out_specs=pl.BlockSpec(block, out_map),
        ),
        out_shape=jax.ShapeDtypeStruct(shape, bf16),
        compiler_params=pltpu.CompilerParams(vmem_limit_bytes=60 << 20),
        cost_estimate=pl.CostEstimate(
            flops=2 * LENGTH * COLS * WIDTH * part // ROWS,
            bytes_accessed=12 << 20,
            transcendentals=0,
        ),
        name=name,
    )(at_x, grouped, x)


def project_b_kernel(place, grouped_ref, x_ref, *outs):
    rows = jnp.concatenate(
        [x_ref[t, :, PART_A:, :].reshape(NZ * PART_B, ROWS) for t in range(8)], axis=1
    )
    res = dot(rows, grouped_ref[...], 1, 0).astype(bf16).reshape(NZ, PART_B, COLS)
    for k, out_ref in enumerate(outs):

        @pl.when(pl.program_id(0) == k)
        def _(out_ref=out_ref):
            out_ref[...] = res


def project_b(at_x, grouped, x):
    shape = (NZ, PART_B, COLS)
    return pl.pallas_call(
        project_b_kernel,
        grid_spec=pltpu.PrefetchScalarGridSpec(
            num_scalar_prefetch=1,
            grid=(NX,),
            in_specs=[
                pl.BlockSpec((LENGTH, COLS), lambda r, place: (0, 0)),
                pl.BlockSpec(
                    (8, NZ, ROWS, ROWS), lambda r, place: (0, lax.rem(place[0] + r, NX), 0, 0)
                ),
            ],
            out_specs=[pl.BlockSpec(shape, lambda r, place: (0, 0, 0))] * NX,
        ),
        out_shape=[jax.ShapeDtypeStruct(shape, bf16)] * NX,
        compiler_params=pltpu.CompilerParams(vmem_limit_bytes=60 << 20),
        cost_estimate=pl.CostEstimate(
            flops=2 * LENGTH * COLS * WIDTH * PART_B // ROWS,
            bytes_accessed=12 << 20,
            transcendentals=0,
        ),
        name="project_b",
    )(at_x, grouped, x)


def fold_kernel(p0, p1, p2, p3, out_ref):
    total = p0[...].astype(f32) + p1[...].astype(f32)
    out_ref[...] = (total + p2[...].astype(f32) + p3[...].astype(f32)).astype(bf16)


def fold(parts):
    spec = pl.BlockSpec((NZ // 4, PART_B, COLS), lambda z: (z, 0, 0))
    return pl.pallas_call(
        fold_kernel,
        grid=(4,),
        in_specs=[spec] * NX,
        out_specs=spec,
        out_shape=jax.ShapeDtypeStruct((NZ, PART_B, COLS), bf16),
        cost_estimate=pl.CostEstimate(flops=0, bytes_accessed=3 << 20, transcendentals=0),
        name="fold",
    )(*parts)


def optimizer_kernel(ga0, ga1, ga2, ga3, gb_ref, w_ref, m_ref, v_ref, m_out, v_out, dir_out, a_out, b_out, sums_out):
    grad_a = ga0[...].astype(f32) + ga1[...].astype(f32)
    grad_a = grad_a + ga2[...].astype(f32) + ga3[...].astype(f32)
    grad_b = jnp.sum(gb_ref[...].astype(f32), axis=0)
    gradient = jnp.concatenate([grad_a, grad_b], axis=0)
    weight = w_ref[...]
    first_new = beta_first * m_ref[...] + (1.0 - beta_first) * gradient
    second_new = beta_second * v_ref[...] + (1.0 - beta_second) * gradient * gradient
    corr_first = 1.0 - beta_first**STEP
    corr_second = 1.0 - beta_second**STEP
    direction = (
        first_new / corr_first / (jnp.sqrt(second_new / corr_second) + adam_epsilon)
        + decay_rate * weight
    )
    m_out[...] = first_new
    v_out[...] = second_new
    dir_out[...] = direction
    a_out[0] = direction[:ROWS_A].astype(bf16)
    a_out[1] = weight[:ROWS_A].astype(bf16)
    b_out[0] = direction[ROWS_A:].astype(bf16)
    b_out[1] = weight[ROWS_A:].astype(bf16)
    weight_sq = jnp.sum(weight * weight)
    update_sq = jnp.sum(direction * direction)
    row = lax.broadcasted_iota(jnp.int32, (8, 128), 0)
    sums_out[...] = jnp.where(row == 0, weight_sq, update_sq)


def optimizer(ga, gb, w, m, v):
    shape = jax.ShapeDtypeStruct((ROWS, COLS), f32)
    return pl.pallas_call(
        optimizer_kernel,
        out_shape=[
            shape,
            shape,
            shape,
            jax.ShapeDtypeStruct((2, ROWS_A, COLS), bf16),
            jax.ShapeDtypeStruct((2, ROWS_B, COLS), bf16),
            jax.ShapeDtypeStruct((8, 128), f32),
        ],
        compiler_params=pltpu.CompilerParams(vmem_limit_bytes=32 << 20),
        name="optimizer",
    )(*ga, gb, w, m, v)


def rate_of(sums_ref):
    sums = jnp.sum(sums_ref[...], axis=0)
    return learn_rate * (jnp.sqrt(sums[0:1, 0:1]) / jnp.sqrt(sums[1:2, 0:1]))


def updated(pair, rate):
    return (pair[1].astype(f32) - rate * pair[0].astype(f32)).astype(bf16)


def apply_a_kernel(place_ref, sums_ref, a0, a1, a2, a3, out_ref):
    rate = rate_of(sums_ref)
    for k, ref in enumerate((a0, a1, a2, a3)):
        out_ref[place_ref[k]] = updated(ref, rate)


def apply_b_kernel(sums_ref, b_ref, out_ref):
    rate = rate_of(sums_ref)
    for z in range(NZ):
        out_ref[z] = updated(b_ref[z], rate)


def apply_step(kernel, operands, count, rows, name):
    vmem = pl.BlockSpec(memory_space=pltpu.VMEM)
    smem = pl.BlockSpec(memory_space=pltpu.SMEM)
    return pl.pallas_call(
        kernel,
        in_specs=[smem if a.ndim == 1 else vmem for a in operands],
        out_specs=vmem,
        out_shape=jax.ShapeDtypeStruct((count, rows, COLS), bf16),
        compiler_params=pltpu.CompilerParams(vmem_limit_bytes=32 << 20),
        name=name,
    )(*operands)


FULL = (NX, NZ, ROWS, COLS)


def join_x_kernel(place_ref, b0, b1, b2, b3, b4, out_ref):
    step, half = pl.program_id(0), pl.program_id(1)
    for k, ref in enumerate((b0, b1, b2)):

        @pl.when(step == k)
        def _(ref=ref):
            out_ref[0] = ref[...]

    for k, ref in enumerate((b3, b4)):

        @pl.when((step == 3) & (half == k))
        def _(ref=ref):
            out_ref[0] = ref[...]


def join_x(place, own, before, after, far_lo, far_hi):
    half = NZ // 2

    def b_spec(k):
        return pl.BlockSpec(
            (half, ROWS_B, COLS),
            lambda o, h, place: (jnp.where(o < k, 0, jnp.where(o > k, 1, h)), 0, 0),
        )

    whole = pl.BlockSpec((half, ROWS_B, COLS), lambda o, h, place: (0, 0, 0))
    return pl.pallas_call(
        join_x_kernel,
        grid_spec=pltpu.PrefetchScalarGridSpec(
            num_scalar_prefetch=1,
            grid=(NX, 2),
            in_specs=[b_spec(0), b_spec(1), b_spec(2), whole, whole],
            out_specs=pl.BlockSpec(
                (1, half, ROWS_B, COLS),
                lambda o, h, place: (place[o], h, ROWS_A // ROWS_B, 0),
            ),
        ),
        out_shape=jax.ShapeDtypeStruct(FULL, bf16),
        compiler_params=pltpu.CompilerParams(vmem_limit_bytes=48 << 20),
        cost_estimate=pl.CostEstimate(flops=0, bytes_accessed=7 << 20, transcendentals=0),
        name="join_x",
    )(place, own, before, after, far_lo, far_hi)


def join_sc_kernel(base_ref, full_ref, out_ref, held, in_sems, out_sems):
    loads, stores = [], []
    for x in range(NX):
        loads.append(pltpu.make_async_copy(full_ref.at[:, x], held.at[x], in_sems.at[x]))
        stores.append(
            pltpu.make_async_copy(
                held.at[x], out_ref.at[x, :, pl.ds(0, ROWS_A), :], out_sems.at[x]
            )
        )
    for load in loads:
        load.start()
    for load, store in zip(loads, stores):
        load.wait()
        store.start()
    for store in stores:
        store.wait()


def join_sc(base, full):
    return pl.pallas_call(
        join_sc_kernel,
        in_specs=[pl.BlockSpec(memory_space=pl.ANY)] * 2,
        out_specs=pl.BlockSpec(memory_space=pl.ANY),
        out_shape=jax.ShapeDtypeStruct(FULL, bf16),
        scratch_shapes=[
            pltpu.VMEM((NX, NZ, ROWS_A, COLS), bf16),
            pltpu.SemaphoreType.DMA((NX,)),
            pltpu.SemaphoreType.DMA((NX,)),
        ],
        input_output_aliases={0: 0},
        compiler_params=pltpu.CompilerParams(vmem_limit_bytes=62 << 20),
        name="join_sc",
    )(base, full)


def shift(value, axis, size, by):
    return lax.ppermute(value, axis, [(i, (i + by) % size) for i in range(size)])


def spread(sums, axes, size):
    wide = jnp.broadcast_to(sums[None], (size,) + sums.shape)
    return lax.all_to_all(wide, axes, 0, 0, tiled=True)


def body(x, q, k, v, g, w, m, s):
    x_turned = turn(x[0])
    packed = pack(q[0], k[0], v[0], g[0])
    heads = lax.all_to_all(packed, ("y", "core"), 0, 0, tiled=True).reshape(LENGTH, PACKED)
    x_full = lax.all_gather(x_turned, ("y", "core"), axis=0, tiled=False)
    grouped = attention(heads)

    at_x = lax.axis_index("x")
    place_x = at_x.reshape(1).astype(jnp.int32)
    part_a = project(grouped, x_full, 0, PART_A, place_x, "project_a")
    part_b = project_b(place_x, grouped, x_full)
    part_a = lax.psum_scatter(part_a, "z", scatter_dimension=0, tiled=True)[0]
    part_b = fold([part_b[0]] + [shift(part_b[by], "x", NX, by) for by in range(1, NX)])
    part_b = lax.all_to_all(part_b, "z", 0, 0, tiled=True)
    part_a = [part_a[0]] + [shift(part_a[by], "x", NX, by) for by in range(1, NX)]

    first_new, second_new, direction, mine_a, mine_b, sums = optimizer(part_a, part_b, w, m, s)
    place = jnp.stack([at_x, (at_x + 3) % NX, (at_x + 1) % NX, (at_x + 2) % NX]).astype(jnp.int32)
    pieces = (
        mine_a,
        shift(mine_a, "x", NX, 1),
        shift(mine_a, "x", NX, -1),
        shift(mine_a, "x", NX, 2),
    )
    gathered_b = lax.all_gather(mine_b, "z", axis=0, tiled=False)
    sums = spread(jnp.sum(spread(sums, ("y", "core"), 8), axis=0), ("x", "z"), 32)
    new_a = apply_step(apply_a_kernel, (place, sums, *pieces), NX, ROWS_A, "apply_a")
    new_b = apply_step(apply_b_kernel, (sums, gathered_b), NZ, ROWS_B, "apply_b")
    full_a = lax.all_gather(new_a, "z", axis=0, tiled=False)
    before, after = shift(new_b, "x", NX, 1), shift(new_b, "x", NX, -1)
    far_lo = shift(before[: NZ // 2], "x", NX, 1)
    far_hi = shift(after[NZ // 2 :], "x", NX, -1)
    new_weights = join_x(place, new_b, before, after, far_lo, far_hi)
    new_weights = join_sc(new_weights, full_a)

    total = jnp.sum(sums, axis=0)
    lamb_update = (jnp.sqrt(total[0, 0]) / jnp.sqrt(total[1, 0])) * direction
    return first_new, second_new, lamb_update, new_weights.reshape(WIDTH, COLS)


def solution(mesh):
    fine = Mesh(mesh.devices.reshape(NX, NZ, NY, NCORE), ("x", "z", "y", "core"))
    dp, ctx = ("x", "z"), ("y", "core")
    seq = P(dp, ctx, None)
    mat = P(dp, ctx)
    return jax.shard_map(
        body,
        mesh=fine,
        in_specs=(seq, seq, seq, seq, seq, mat, mat, mat),
        out_specs=(mat, mat, mat, P(None, ctx)),
        check_vma=False,
    )
```

```python
import jax
import jax.numpy as jnp
from jax import lax
from jax.experimental import pallas as pl
from jax.experimental.pallas import tpu as pltpu
from jax.sharding import Mesh
from jax.sharding import PartitionSpec as P

HEAD_DIM = 128
STEP = 100
GROUP = 4
NX, NZ, NY, NCORE = 4, 8, 4, 2
LENGTH = 1024
COLS = 768
WIDTH = 4096
ROWS = 128
PACKED = 1280
BLOCK = 256
PART_A = 80
PART_B = ROWS - PART_A
ROWS_A = 48
ROWS_B = ROWS - ROWS_A

beta_first = 0.9
beta_second = 0.999
adam_epsilon = 1e-06
decay_rate = 0.01
learn_rate = 0.01
masked_score = -1e30
score_scale = HEAD_DIM ** (-0.5)
LOG2E = 1.4426950408889634

f32 = jnp.float32
bf16 = jnp.bfloat16


def dot(a, b, ca, cb):
    return lax.dot_general(a, b, (((ca,), (cb,)), ((), ())), preferred_element_type=f32)


def pack_kernel(q_ref, k_ref, v_ref, g_ref, out_ref):
    for c in range(out_ref.shape[0]):
        out_ref[c, :, 0:512] = q_ref[:, c * 512 : (c + 1) * 512]
        out_ref[c, :, 512:640] = k_ref[:, c * 128 : (c + 1) * 128]
        out_ref[c, :, 640:768] = v_ref[:, c * 128 : (c + 1) * 128]
        out_ref[c, :, 768:1280] = g_ref[:, c * 512 : (c + 1) * 512]


def pack(q, k, v, g):
    rows = q.shape[0]
    each = 4
    return pl.pallas_call(
        pack_kernel,
        grid=(8 // each,),
        in_specs=[
            pl.BlockSpec((rows, 512 * each), lambda c: (0, c)),
            pl.BlockSpec((rows, 128 * each), lambda c: (0, c)),
            pl.BlockSpec((rows, 128 * each), lambda c: (0, c)),
            pl.BlockSpec((rows, 512 * each), lambda c: (0, c)),
        ],
        out_specs=pl.BlockSpec((each, rows, PACKED), lambda c: (c, 0, 0)),
        out_shape=jax.ShapeDtypeStruct((8, rows, PACKED), bf16),
        cost_estimate=pl.CostEstimate(flops=0, bytes_accessed=5 << 20, transcendentals=0),
        name="pack",
    )(q, k, v, g)


def turn_kernel(x_ref, out_ref):
    for i in range(out_ref.shape[0]):
        out_ref[i] = x_ref[:, i * ROWS : (i + 1) * ROWS].T


def turn(x):
    tokens = x.shape[0]
    each = 16
    return pl.pallas_call(
        turn_kernel,
        grid=(NX * NZ // each,),
        in_specs=[pl.BlockSpec((tokens, ROWS * each), lambda i: (0, i))],
        out_specs=pl.BlockSpec((each, ROWS, tokens), lambda i: (i, 0, 0)),
        out_shape=jax.ShapeDtypeStruct((NX * NZ, ROWS, tokens), bf16),
        cost_estimate=pl.CostEstimate(flops=0, bytes_accessed=2 << 20, transcendentals=0),
        name="turn",
    )(x)


def attention_kernel(q_ref, k_ref, v_ref, g_ref, out_ref, kt_ref, dk_acc, dv_acc):
    head = pl.program_id(0)

    @pl.when(head == 0)
    def _():
        kt_ref[...] = k_ref[...].T
        dk_acc[...] = jnp.zeros_like(dk_acc)
        dv_acc[...] = jnp.zeros_like(dv_acc)

    key_pos = lax.broadcasted_iota(jnp.int32, (BLOCK, BLOCK), 0)
    query_pos = lax.broadcasted_iota(jnp.int32, (BLOCK, BLOCK), 1)
    allowed = key_pos <= query_pos
    for i in range(LENGTH // BLOCK):
        lo, hi = i * BLOCK, (i + 1) * BLOCK
        q = q_ref[lo:hi, :]
        g = g_ref[lo:hi, :]
        scores = dot(k_ref[:hi, :], q, 1, 1)
        diag = jnp.where(allowed, scores[lo:hi, :], masked_score)
        scores = diag if i == 0 else jnp.concatenate([scores[:lo, :], diag], axis=0)
        top = jnp.max(scores, axis=0, keepdims=True)
        weights = jnp.exp2((scores - top) * (score_scale * LOG2E))
        probs = weights * (1.0 / jnp.sum(weights, axis=0, keepdims=True))
        probs_b = probs.astype(bf16)
        prob_grad = dot(v_ref[:hi, :], g, 1, 1)
        row_delta = jnp.sum(probs_b.astype(f32) * prob_grad, axis=0, keepdims=True)
        dscore = (probs * (prob_grad - row_delta)).astype(bf16)
        dq_t = dot(kt_ref[:, :hi], dscore, 1, 0) * score_scale
        out_ref[lo:hi, pl.ds(pl.multiple_of(head * 128, 128), 128)] = dq_t.astype(bf16).T
        dk_acc[:hi, :] += dot(dscore, q, 1, 0)
        dv_acc[:hi, :] += dot(probs_b, g, 1, 0)

    @pl.when(head == GROUP - 1)
    def _():
        out_ref[:, 512:640] = (dk_acc[...] * score_scale).astype(bf16)
        out_ref[:, 640:768] = dv_acc[...].astype(bf16)


def attention(packed):
    return pl.pallas_call(
        attention_kernel,
        grid=(GROUP,),
        in_specs=[
            pl.BlockSpec((LENGTH, 128), lambda h: (0, h)),
            pl.BlockSpec((LENGTH, 128), lambda h: (0, 4)),
            pl.BlockSpec((LENGTH, 128), lambda h: (0, 5)),
            pl.BlockSpec((LENGTH, 128), lambda h: (0, 6 + h)),
        ],
        out_specs=pl.BlockSpec((LENGTH, COLS), lambda h: (0, 0)),
        out_shape=jax.ShapeDtypeStruct((LENGTH, COLS), bf16),
        scratch_shapes=[
            pltpu.VMEM((128, LENGTH), bf16),
            pltpu.VMEM((LENGTH, 128), f32),
            pltpu.VMEM((LENGTH, 128), f32),
        ],
        compiler_params=pltpu.CompilerParams(vmem_limit_bytes=48 << 20),
        cost_estimate=pl.CostEstimate(
            flops=4 << 30, bytes_accessed=5 << 20, transcendentals=4 << 20
        ),
        name="attention_backward",
    )(packed, packed, packed, packed)


def project(grouped, x, lo, hi, at_x, name):
    part = hi - lo

    def kernel(place, grouped_ref, x_ref, out_ref):
        rows = jnp.concatenate(
            [x_ref[t, :, lo:hi, :].reshape(NZ * part, ROWS) for t in range(8)], axis=1
        )
        res = dot(rows, grouped_ref[...], 1, 0).astype(bf16)
        out_ref[...] = res.reshape(out_ref.shape)

    if at_x is None:
        shape, block = (NX, NZ, part, COLS), (1, NZ, part, COLS)
        out_map = lambda x, place: (x, 0, 0, 0)
        at_x = jnp.zeros((1,), jnp.int32)
    else:
        shape, block = (NZ, NX, part, COLS), (NZ, 1, part, COLS)
        out_map = lambda x, place: (0, lax.rem(x - place[0] + NX, NX), 0, 0)
    return pl.pallas_call(
        kernel,
        grid_spec=pltpu.PrefetchScalarGridSpec(
            num_scalar_prefetch=1,
            grid=(NX,),
            in_specs=[
                pl.BlockSpec((LENGTH, COLS), lambda x, place: (0, 0)),
                pl.BlockSpec((8, NZ, ROWS, ROWS), lambda x, place: (0, x, 0, 0)),
            ],
            out_specs=pl.BlockSpec(block, out_map),
        ),
        out_shape=jax.ShapeDtypeStruct(shape, bf16),
        compiler_params=pltpu.CompilerParams(vmem_limit_bytes=60 << 20),
        cost_estimate=pl.CostEstimate(
            flops=2 * LENGTH * COLS * WIDTH * part // ROWS,
            bytes_accessed=12 << 20,
            transcendentals=0,
        ),
        name=name,
    )(at_x, grouped, x)


def project_b_kernel(place, grouped_ref, x_ref, *outs):
    rows = jnp.concatenate(
        [x_ref[t, :, PART_A:, :].reshape(NZ * PART_B, ROWS) for t in range(8)], axis=1
    )
    res = dot(rows, grouped_ref[...], 1, 0).astype(bf16).reshape(NZ, PART_B, COLS)
    for k, out_ref in enumerate(outs):

        @pl.when(pl.program_id(0) == k)
        def _(out_ref=out_ref):
            out_ref[...] = res


def project_b(at_x, grouped, x):
    shape = (NZ, PART_B, COLS)
    return pl.pallas_call(
        project_b_kernel,
        grid_spec=pltpu.PrefetchScalarGridSpec(
            num_scalar_prefetch=1,
            grid=(NX,),
            in_specs=[
                pl.BlockSpec((LENGTH, COLS), lambda r, place: (0, 0)),
                pl.BlockSpec(
                    (8, NZ, ROWS, ROWS), lambda r, place: (0, lax.rem(place[0] + r, NX), 0, 0)
                ),
            ],
            out_specs=[pl.BlockSpec(shape, lambda r, place: (0, 0, 0))] * NX,
        ),
        out_shape=[jax.ShapeDtypeStruct(shape, bf16)] * NX,
        compiler_params=pltpu.CompilerParams(vmem_limit_bytes=60 << 20),
        cost_estimate=pl.CostEstimate(
            flops=2 * LENGTH * COLS * WIDTH * PART_B // ROWS,
            bytes_accessed=12 << 20,
            transcendentals=0,
        ),
        name="project_b",
    )(at_x, grouped, x)


def fold_kernel(p0, p1, p2, p3, out_ref):
    total = p0[...].astype(f32) + p1[...].astype(f32)
    out_ref[...] = (total + p2[...].astype(f32) + p3[...].astype(f32)).astype(bf16)


def fold(parts):
    spec = pl.BlockSpec((NZ // 4, PART_B, COLS), lambda z: (z, 0, 0))
    return pl.pallas_call(
        fold_kernel,
        grid=(4,),
        in_specs=[spec] * NX,
        out_specs=spec,
        out_shape=jax.ShapeDtypeStruct((NZ, PART_B, COLS), bf16),
        cost_estimate=pl.CostEstimate(flops=0, bytes_accessed=3 << 20, transcendentals=0),
        name="fold",
    )(*parts)


def optimizer_kernel(ga0, ga1, ga2, ga3, gb_ref, w_ref, m_ref, v_ref, m_out, v_out, dir_out, a_out, b_out, sums_out):
    grad_a = ga0[...].astype(f32) + ga1[...].astype(f32)
    grad_a = grad_a + ga2[...].astype(f32) + ga3[...].astype(f32)
    grad_b = jnp.sum(gb_ref[...].astype(f32), axis=0)
    gradient = jnp.concatenate([grad_a, grad_b], axis=0)
    weight = w_ref[...]
    first_new = beta_first * m_ref[...] + (1.0 - beta_first) * gradient
    second_new = beta_second * v_ref[...] + (1.0 - beta_second) * gradient * gradient
    corr_first = 1.0 - beta_first**STEP
    corr_second = 1.0 - beta_second**STEP
    direction = (
        first_new / corr_first / (jnp.sqrt(second_new / corr_second) + adam_epsilon)
        + decay_rate * weight
    )
    m_out[...] = first_new
    v_out[...] = second_new
    dir_out[...] = direction
    a_out[0] = direction[ROWS_B:].astype(bf16)
    a_out[1] = weight[ROWS_B:].astype(bf16)
    b_out[0] = direction[:ROWS_B].astype(bf16)
    b_out[1] = weight[:ROWS_B].astype(bf16)
    weight_sq = jnp.sum(weight * weight)
    update_sq = jnp.sum(direction * direction)
    row = lax.broadcasted_iota(jnp.int32, (8, 128), 0)
    sums_out[...] = jnp.where(row == 0, weight_sq, update_sq)


def optimizer(ga, gb, w, m, v):
    shape = jax.ShapeDtypeStruct((ROWS, COLS), f32)
    return pl.pallas_call(
        optimizer_kernel,
        out_shape=[
            shape,
            shape,
            shape,
            jax.ShapeDtypeStruct((2, ROWS_A, COLS), bf16),
            jax.ShapeDtypeStruct((2, ROWS_B, COLS), bf16),
            jax.ShapeDtypeStruct((8, 128), f32),
        ],
        compiler_params=pltpu.CompilerParams(vmem_limit_bytes=32 << 20),
        name="optimizer",
    )(*ga, gb, w, m, v)


def rate_of(sums_ref):
    sums = jnp.sum(sums_ref[...], axis=0)
    return learn_rate * (jnp.sqrt(sums[0:1, 0:1]) / jnp.sqrt(sums[1:2, 0:1]))


def updated(pair, rate):
    return (pair[1].astype(f32) - rate * pair[0].astype(f32)).astype(bf16)


def apply_a_kernel(place_ref, sums_ref, a0, a1, a2, a3, out_ref):
    rate = rate_of(sums_ref)
    for k, ref in enumerate((a0, a1, a2, a3)):
        out_ref[place_ref[k]] = updated(ref, rate)


def apply_b_kernel(sums_ref, b_ref, out_ref):
    rate = rate_of(sums_ref)
    for z in range(NZ):
        out_ref[z] = updated(b_ref[z], rate)


def apply_step(kernel, operands, count, rows, name):
    vmem = pl.BlockSpec(memory_space=pltpu.VMEM)
    smem = pl.BlockSpec(memory_space=pltpu.SMEM)
    return pl.pallas_call(
        kernel,
        in_specs=[smem if a.ndim == 1 else vmem for a in operands],
        out_specs=vmem,
        out_shape=jax.ShapeDtypeStruct((count, rows, COLS), bf16),
        compiler_params=pltpu.CompilerParams(vmem_limit_bytes=32 << 20),
        name=name,
    )(*operands)


FULL = (NX, NZ, ROWS, COLS)


def join_x_kernel(place_ref, b0, b1, b2, b3, b4, out_ref):
    step, half = pl.program_id(0), pl.program_id(1)
    for k, ref in enumerate((b0, b1, b2)):

        @pl.when(step == k)
        def _(ref=ref):
            out_ref[0] = ref[...]

    for k, ref in enumerate((b3, b4)):

        @pl.when((step == 3) & (half == k))
        def _(ref=ref):
            out_ref[0] = ref[...]


def join_x(place, own, before, after, far_lo, far_hi):
    half = NZ // 2

    def b_spec(k):
        return pl.BlockSpec(
            (half, ROWS_B, COLS),
            lambda o, h, place: (jnp.where(o < k, 0, jnp.where(o > k, 1, h)), 0, 0),
        )

    whole = pl.BlockSpec((half, ROWS_B, COLS), lambda o, h, place: (0, 0, 0))
    return pl.pallas_call(
        join_x_kernel,
        grid_spec=pltpu.PrefetchScalarGridSpec(
            num_scalar_prefetch=1,
            grid=(NX, 2),
            in_specs=[b_spec(0), b_spec(1), b_spec(2), whole, whole],
            out_specs=pl.BlockSpec(
                (1, half, ROWS_B, COLS),
                lambda o, h, place: (place[o], h, 0, 0),
            ),
        ),
        out_shape=jax.ShapeDtypeStruct(FULL, bf16),
        compiler_params=pltpu.CompilerParams(vmem_limit_bytes=48 << 20),
        cost_estimate=pl.CostEstimate(flops=0, bytes_accessed=7 << 20, transcendentals=0),
        name="join_x",
    )(place, own, before, after, far_lo, far_hi)


def join_sc_kernel(base_ref, full_ref, out_ref, held, in_sems, out_sems):
    loads, stores = [], []
    for x in range(NX):
        loads.append(pltpu.make_async_copy(full_ref.at[:, x], held.at[x], in_sems.at[x]))
        stores.append(
            pltpu.make_async_copy(
                held.at[x], out_ref.at[x, :, pl.ds(ROWS_B, ROWS_A), :], out_sems.at[x]
            )
        )
    for load in loads:
        load.start()
    for load, store in zip(loads, stores):
        load.wait()
        store.start()
    for store in stores:
        store.wait()


def join_sc(base, full):
    return pl.pallas_call(
        join_sc_kernel,
        in_specs=[pl.BlockSpec(memory_space=pl.ANY)] * 2,
        out_specs=pl.BlockSpec(memory_space=pl.ANY),
        out_shape=jax.ShapeDtypeStruct(FULL, bf16),
        scratch_shapes=[
            pltpu.VMEM((NX, NZ, ROWS_A, COLS), bf16),
            pltpu.SemaphoreType.DMA((NX,)),
            pltpu.SemaphoreType.DMA((NX,)),
        ],
        input_output_aliases={0: 0},
        compiler_params=pltpu.CompilerParams(vmem_limit_bytes=62 << 20),
        name="join_sc",
    )(base, full)


def shift(value, axis, size, by):
    return lax.ppermute(value, axis, [(i, (i + by) % size) for i in range(size)])


def spread(sums, axes, size):
    wide = jnp.broadcast_to(sums[None], (size,) + sums.shape)
    return lax.all_to_all(wide, axes, 0, 0, tiled=True)


def body(x, q, k, v, g, w, m, s):
    x_turned = turn(x[0])
    packed = pack(q[0], k[0], v[0], g[0])
    heads = lax.all_to_all(packed, ("y", "core"), 0, 0, tiled=True).reshape(LENGTH, PACKED)
    x_full = lax.all_gather(x_turned, ("y", "core"), axis=0, tiled=False)
    grouped = attention(heads)

    at_x = lax.axis_index("x")
    place_x = at_x.reshape(1).astype(jnp.int32)
    part_a = project(grouped, x_full, 0, PART_A, place_x, "project_a")
    part_b = project_b(place_x, grouped, x_full)
    part_a = lax.psum_scatter(part_a, "z", scatter_dimension=0, tiled=True)[0]
    part_b = fold([part_b[0]] + [shift(part_b[by], "x", NX, by) for by in range(1, NX)])
    part_b = lax.all_to_all(part_b, "z", 0, 0, tiled=True)
    part_a = [part_a[0]] + [shift(part_a[by], "x", NX, by) for by in range(1, NX)]

    first_new, second_new, direction, mine_a, mine_b, sums = optimizer(part_a, part_b, w, m, s)
    place = jnp.stack([at_x, (at_x + 3) % NX, (at_x + 1) % NX, (at_x + 2) % NX]).astype(jnp.int32)
    pieces = (
        mine_a,
        shift(mine_a, "x", NX, 1),
        shift(mine_a, "x", NX, -1),
        shift(mine_a, "x", NX, 2),
    )
    gathered_b = lax.all_gather(mine_b, "z", axis=0, tiled=False)
    sums = spread(jnp.sum(spread(sums, ("y", "core"), 8), axis=0), ("x", "z"), 32)
    new_a = apply_step(apply_a_kernel, (place, sums, *pieces), NX, ROWS_A, "apply_a")
    new_b = apply_step(apply_b_kernel, (sums, gathered_b), NZ, ROWS_B, "apply_b")
    full_a = lax.all_gather(new_a, "z", axis=0, tiled=False)
    before, after = shift(new_b, "x", NX, 1), shift(new_b, "x", NX, -1)
    far_lo = shift(before[: NZ // 2], "x", NX, 1)
    far_hi = shift(after[NZ // 2 :], "x", NX, -1)
    new_weights = join_x(place, new_b, before, after, far_lo, far_hi)
    new_weights = join_sc(new_weights, full_a)

    total = jnp.sum(sums, axis=0)
    lamb_update = (jnp.sqrt(total[0, 0]) / jnp.sqrt(total[1, 0])) * direction
    return first_new, second_new, lamb_update, new_weights.reshape(WIDTH, COLS)


def solution(mesh):
    fine = Mesh(mesh.devices.reshape(NX, NZ, NY, NCORE), ("x", "z", "y", "core"))
    dp, ctx = ("x", "z"), ("y", "core")
    seq = P(dp, ctx, None)
    mat = P(dp, ctx)
    return jax.shard_map(
        body,
        mesh=fine,
        in_specs=(seq, seq, seq, seq, seq, mat, mat, mat),
        out_specs=(mat, mat, mat, P(None, ctx)),
        check_vma=False,
    )
```

```python
import jax
import jax.numpy as jnp
from jax import lax
from jax.experimental import pallas as pl
from jax.experimental.pallas import tpu as pltpu
from jax.sharding import Mesh
from jax.sharding import PartitionSpec as P

HEAD_DIM = 128
STEP = 100
GROUP = 4
NX, NZ, NY, NCORE = 4, 8, 4, 2
LENGTH = 1024
COLS = 768
WIDTH = 4096
ROWS = 128
PACKED = 1280
BLOCK = 256
PART_A = 80
PART_B = ROWS - PART_A
ROWS_A = 48
ROWS_B = ROWS - ROWS_A

beta_first = 0.9
beta_second = 0.999
adam_epsilon = 1e-06
decay_rate = 0.01
learn_rate = 0.01
masked_score = -1e30
score_scale = HEAD_DIM ** (-0.5)
LOG2E = 1.4426950408889634

f32 = jnp.float32
bf16 = jnp.bfloat16


def dot(a, b, ca, cb):
    return lax.dot_general(a, b, (((ca,), (cb,)), ((), ())), preferred_element_type=f32)


def pack_kernel(q_ref, k_ref, v_ref, g_ref, out_ref):
    for c in range(out_ref.shape[0]):
        out_ref[c, :, 0:512] = q_ref[:, c * 512 : (c + 1) * 512]
        out_ref[c, :, 512:640] = k_ref[:, c * 128 : (c + 1) * 128]
        out_ref[c, :, 640:768] = v_ref[:, c * 128 : (c + 1) * 128]
        out_ref[c, :, 768:1280] = g_ref[:, c * 512 : (c + 1) * 512]


def pack(q, k, v, g):
    rows = q.shape[0]
    each = 4
    return pl.pallas_call(
        pack_kernel,
        grid=(8 // each,),
        in_specs=[
            pl.BlockSpec((rows, 512 * each), lambda c: (0, c)),
            pl.BlockSpec((rows, 128 * each), lambda c: (0, c)),
            pl.BlockSpec((rows, 128 * each), lambda c: (0, c)),
            pl.BlockSpec((rows, 512 * each), lambda c: (0, c)),
        ],
        out_specs=pl.BlockSpec((each, rows, PACKED), lambda c: (c, 0, 0)),
        out_shape=jax.ShapeDtypeStruct((8, rows, PACKED), bf16),
        cost_estimate=pl.CostEstimate(flops=0, bytes_accessed=5 << 20, transcendentals=0),
        name="pack",
    )(q, k, v, g)


def turn_kernel(x_ref, out_ref):
    for i in range(out_ref.shape[0]):
        out_ref[i] = x_ref[:, i * ROWS : (i + 1) * ROWS].T


def turn(x):
    tokens = x.shape[0]
    each = 16
    return pl.pallas_call(
        turn_kernel,
        grid=(NX * NZ // each,),
        in_specs=[pl.BlockSpec((tokens, ROWS * each), lambda i: (0, i))],
        out_specs=pl.BlockSpec((each, ROWS, tokens), lambda i: (i, 0, 0)),
        out_shape=jax.ShapeDtypeStruct((NX * NZ, ROWS, tokens), bf16),
        cost_estimate=pl.CostEstimate(flops=0, bytes_accessed=2 << 20, transcendentals=0),
        name="turn",
    )(x)


def attention_kernel(q_ref, k_ref, v_ref, g_ref, out_ref, kt_ref, dk_acc, dv_acc):
    head = pl.program_id(0)

    @pl.when(head == 0)
    def _():
        kt_ref[...] = k_ref[...].T
        dk_acc[...] = jnp.zeros_like(dk_acc)
        dv_acc[...] = jnp.zeros_like(dv_acc)

    key_pos = lax.broadcasted_iota(jnp.int32, (BLOCK, BLOCK), 0)
    query_pos = lax.broadcasted_iota(jnp.int32, (BLOCK, BLOCK), 1)
    allowed = key_pos <= query_pos
    for i in range(LENGTH // BLOCK):
        lo, hi = i * BLOCK, (i + 1) * BLOCK
        q = q_ref[lo:hi, :]
        g = g_ref[lo:hi, :]
        scores = dot(k_ref[:hi, :], q, 1, 1)
        diag = jnp.where(allowed, scores[lo:hi, :], masked_score)
        scores = diag if i == 0 else jnp.concatenate([scores[:lo, :], diag], axis=0)
        top = jnp.max(scores, axis=0, keepdims=True)
        weights = jnp.exp2((scores - top) * (score_scale * LOG2E))
        probs = weights * (1.0 / jnp.sum(weights, axis=0, keepdims=True))
        probs_b = probs.astype(bf16)
        prob_grad = dot(v_ref[:hi, :], g, 1, 1)
        row_delta = jnp.sum(probs_b.astype(f32) * prob_grad, axis=0, keepdims=True)
        dscore = (probs * (prob_grad - row_delta)).astype(bf16)
        dq_t = dot(kt_ref[:, :hi], dscore, 1, 0) * score_scale
        out_ref[lo:hi, pl.ds(pl.multiple_of(head * 128, 128), 128)] = dq_t.astype(bf16).T
        dk_acc[:hi, :] += dot(dscore, q, 1, 0)
        dv_acc[:hi, :] += dot(probs_b, g, 1, 0)

    @pl.when(head == GROUP - 1)
    def _():
        out_ref[:, 512:640] = (dk_acc[...] * score_scale).astype(bf16)
        out_ref[:, 640:768] = dv_acc[...].astype(bf16)


def attention(packed):
    return pl.pallas_call(
        attention_kernel,
        grid=(GROUP,),
        in_specs=[
            pl.BlockSpec((LENGTH, 128), lambda h: (0, h)),
            pl.BlockSpec((LENGTH, 128), lambda h: (0, 4)),
            pl.BlockSpec((LENGTH, 128), lambda h: (0, 5)),
            pl.BlockSpec((LENGTH, 128), lambda h: (0, 6 + h)),
        ],
        out_specs=pl.BlockSpec((LENGTH, COLS), lambda h: (0, 0)),
        out_shape=jax.ShapeDtypeStruct((LENGTH, COLS), bf16),
        scratch_shapes=[
            pltpu.VMEM((128, LENGTH), bf16),
            pltpu.VMEM((LENGTH, 128), f32),
            pltpu.VMEM((LENGTH, 128), f32),
        ],
        compiler_params=pltpu.CompilerParams(vmem_limit_bytes=48 << 20),
        cost_estimate=pl.CostEstimate(
            flops=4 << 30, bytes_accessed=5 << 20, transcendentals=4 << 20
        ),
        name="attention_backward",
    )(packed, packed, packed, packed)


def project_a_kernel(place, grouped_ref, x0, x1, out_ref):
    for k, ref in enumerate((x0, x1)):
        rows = jnp.concatenate(
            [ref[t, :, :PART_A, :].reshape(NZ * PART_A, ROWS) for t in range(8)], axis=1
        )
        if k == 0:
            first = rows
    rows = jnp.concatenate([first, rows], axis=0)
    res = dot(rows, grouped_ref[...], 1, 0).astype(bf16).reshape(2, NZ, PART_A, COLS)
    out_ref[:, 0] = res[0]
    out_ref[:, 1] = res[1]


def project_a(at_x, grouped, x):
    def x_spec(by):
        return pl.BlockSpec(
            (8, NZ, ROWS, ROWS), lambda j, place: (0, lax.rem(place[0] + 2 * j + by, NX), 0, 0)
        )

    return pl.pallas_call(
        project_a_kernel,
        grid_spec=pltpu.PrefetchScalarGridSpec(
            num_scalar_prefetch=1,
            grid=(NX // 2,),
            in_specs=[
                pl.BlockSpec((LENGTH, COLS), lambda j, place: (0, 0)),
                x_spec(0),
                x_spec(1),
            ],
            out_specs=pl.BlockSpec((NZ, 2, PART_A, COLS), lambda j, place: (0, j, 0, 0)),
        ),
        out_shape=jax.ShapeDtypeStruct((NZ, NX, PART_A, COLS), bf16),
        compiler_params=pltpu.CompilerParams(vmem_limit_bytes=60 << 20),
        cost_estimate=pl.CostEstimate(
            flops=2 * LENGTH * COLS * WIDTH * PART_A // ROWS,
            bytes_accessed=12 << 20,
            transcendentals=0,
        ),
        name="project_a",
    )(at_x, grouped, x, x)


def project_b_kernel(place, grouped_ref, x_ref, *outs):
    rows = jnp.concatenate(
        [x_ref[t, :, PART_A:, :].reshape(NZ * PART_B, ROWS) for t in range(8)], axis=1
    )
    res = dot(rows, grouped_ref[...], 1, 0).astype(bf16).reshape(NZ, PART_B, COLS)
    for k, out_ref in enumerate(outs):

        @pl.when(pl.program_id(0) == k)
        def _(out_ref=out_ref):
            out_ref[...] = res


def project_b(at_x, grouped, x):
    shape = (NZ, PART_B, COLS)
    return pl.pallas_call(
        project_b_kernel,
        grid_spec=pltpu.PrefetchScalarGridSpec(
            num_scalar_prefetch=1,
            grid=(NX,),
            in_specs=[
                pl.BlockSpec((LENGTH, COLS), lambda r, place: (0, 0)),
                pl.BlockSpec(
                    (8, NZ, ROWS, ROWS), lambda r, place: (0, lax.rem(place[0] + r, NX), 0, 0)
                ),
            ],
            out_specs=[pl.BlockSpec(shape, lambda r, place: (0, 0, 0))] * NX,
        ),
        out_shape=[jax.ShapeDtypeStruct(shape, bf16)] * NX,
        compiler_params=pltpu.CompilerParams(vmem_limit_bytes=60 << 20),
        cost_estimate=pl.CostEstimate(
            flops=2 * LENGTH * COLS * WIDTH * PART_B // ROWS,
            bytes_accessed=12 << 20,
            transcendentals=0,
        ),
        name="project_b",
    )(at_x, grouped, x)


def fold_kernel(p0, p1, p2, p3, out_ref):
    total = p0[...].astype(f32) + p1[...].astype(f32)
    out_ref[...] = (total + p2[...].astype(f32) + p3[...].astype(f32)).astype(bf16)


def fold(parts):
    spec = pl.BlockSpec((NZ // 4, PART_B, COLS), lambda z: (z, 0, 0))
    return pl.pallas_call(
        fold_kernel,
        grid=(4,),
        in_specs=[spec] * NX,
        out_specs=spec,
        out_shape=jax.ShapeDtypeStruct((NZ, PART_B, COLS), bf16),
        cost_estimate=pl.CostEstimate(flops=0, bytes_accessed=3 << 20, transcendentals=0),
        name="fold",
    )(*parts)


def optimizer_kernel(ga0, ga1, ga2, ga3, gb_ref, w_ref, m_ref, v_ref, m_out, v_out, dir_out, a_out, b_out, sums_out):
    grad_a = ga0[...].astype(f32) + ga1[...].astype(f32)
    grad_a = grad_a + ga2[...].astype(f32) + ga3[...].astype(f32)
    grad_b = jnp.sum(gb_ref[...].astype(f32), axis=0)
    gradient = jnp.concatenate([grad_a, grad_b], axis=0)
    weight = w_ref[...]
    first_new = beta_first * m_ref[...] + (1.0 - beta_first) * gradient
    second_new = beta_second * v_ref[...] + (1.0 - beta_second) * gradient * gradient
    corr_first = 1.0 - beta_first**STEP
    corr_second = 1.0 - beta_second**STEP
    direction = (
        first_new / corr_first / (jnp.sqrt(second_new / corr_second) + adam_epsilon)
        + decay_rate * weight
    )
    m_out[...] = first_new
    v_out[...] = second_new
    dir_out[...] = direction
    a_out[0] = direction[ROWS_B:].astype(bf16)
    a_out[1] = weight[ROWS_B:].astype(bf16)
    b_out[0] = direction[:ROWS_B].astype(bf16)
    b_out[1] = weight[:ROWS_B].astype(bf16)
    weight_sq = jnp.sum(weight * weight)
    update_sq = jnp.sum(direction * direction)
    row = lax.broadcasted_iota(jnp.int32, (8, 128), 0)
    sums_out[...] = jnp.where(row == 0, weight_sq, update_sq)


def optimizer(ga, gb, w, m, v):
    shape = jax.ShapeDtypeStruct((ROWS, COLS), f32)
    return pl.pallas_call(
        optimizer_kernel,
        out_shape=[
            shape,
            shape,
            shape,
            jax.ShapeDtypeStruct((2, ROWS_A, COLS), bf16),
            jax.ShapeDtypeStruct((2, ROWS_B, COLS), bf16),
            jax.ShapeDtypeStruct((8, 128), f32),
        ],
        compiler_params=pltpu.CompilerParams(vmem_limit_bytes=32 << 20),
        name="optimizer",
    )(*ga, gb, w, m, v)


def rate_of(sums_ref):
    sums = jnp.sum(sums_ref[...], axis=0)
    return learn_rate * (jnp.sqrt(sums[0:1, 0:1]) / jnp.sqrt(sums[1:2, 0:1]))


def updated(pair, rate):
    return (pair[1].astype(f32) - rate * pair[0].astype(f32)).astype(bf16)


def apply_a_kernel(place_ref, sums_ref, a0, a1, a2, a3, out_ref):
    rate = rate_of(sums_ref)
    for k, ref in enumerate((a0, a1, a2, a3)):
        out_ref[place_ref[k]] = updated(ref, rate)


def apply_b_kernel(sums_ref, b_ref, out_ref):
    rate = rate_of(sums_ref)
    for z in range(NZ):
        out_ref[z] = updated(b_ref[z], rate)


def apply_step(kernel, operands, count, rows, name):
    vmem = pl.BlockSpec(memory_space=pltpu.VMEM)
    smem = pl.BlockSpec(memory_space=pltpu.SMEM)
    return pl.pallas_call(
        kernel,
        in_specs=[smem if a.ndim == 1 else vmem for a in operands],
        out_specs=vmem,
        out_shape=jax.ShapeDtypeStruct((count, rows, COLS), bf16),
        compiler_params=pltpu.CompilerParams(vmem_limit_bytes=32 << 20),
        name=name,
    )(*operands)


FULL = (NX, NZ, ROWS, COLS)


def join_x_kernel(place_ref, b0, b1, b2, b3, b4, out_ref):
    step, half = pl.program_id(0), pl.program_id(1)
    for k, ref in enumerate((b0, b1, b2)):

        @pl.when(step == k)
        def _(ref=ref):
            out_ref[0] = ref[...]

    for k, ref in enumerate((b3, b4)):

        @pl.when((step == 3) & (half == k))
        def _(ref=ref):
            out_ref[0] = ref[...]


def join_x(place, own, before, after, far_lo, far_hi):
    half = NZ // 2

    def b_spec(k):
        return pl.BlockSpec(
            (half, ROWS_B, COLS),
            lambda o, h, place: (jnp.where(o < k, 0, jnp.where(o > k, 1, h)), 0, 0),
        )

    whole = pl.BlockSpec((half, ROWS_B, COLS), lambda o, h, place: (0, 0, 0))
    return pl.pallas_call(
        join_x_kernel,
        grid_spec=pltpu.PrefetchScalarGridSpec(
            num_scalar_prefetch=1,
            grid=(NX, 2),
            in_specs=[b_spec(0), b_spec(1), b_spec(2), whole, whole],
            out_specs=pl.BlockSpec(
                (1, half, ROWS_B, COLS),
                lambda o, h, place: (place[o], h, 0, 0),
            ),
        ),
        out_shape=jax.ShapeDtypeStruct(FULL, bf16),
        compiler_params=pltpu.CompilerParams(vmem_limit_bytes=48 << 20),
        cost_estimate=pl.CostEstimate(flops=0, bytes_accessed=7 << 20, transcendentals=0),
        name="join_x",
    )(place, own, before, after, far_lo, far_hi)


def join_sc_kernel(base_ref, full_ref, out_ref, held, in_sems, out_sems):
    loads, stores = [], []
    for x in range(NX):
        loads.append(pltpu.make_async_copy(full_ref.at[:, x], held.at[x], in_sems.at[x]))
        stores.append(
            pltpu.make_async_copy(
                held.at[x], out_ref.at[x, :, pl.ds(ROWS_B, ROWS_A), :], out_sems.at[x]
            )
        )
    for load in loads:
        load.start()
    for load, store in zip(loads, stores):
        load.wait()
        store.start()
    for store in stores:
        store.wait()


def join_sc(base, full):
    return pl.pallas_call(
        join_sc_kernel,
        in_specs=[pl.BlockSpec(memory_space=pl.ANY)] * 2,
        out_specs=pl.BlockSpec(memory_space=pl.ANY),
        out_shape=jax.ShapeDtypeStruct(FULL, bf16),
        scratch_shapes=[
            pltpu.VMEM((NX, NZ, ROWS_A, COLS), bf16),
            pltpu.SemaphoreType.DMA((NX,)),
            pltpu.SemaphoreType.DMA((NX,)),
        ],
        input_output_aliases={0: 0},
        compiler_params=pltpu.CompilerParams(vmem_limit_bytes=62 << 20),
        name="join_sc",
    )(base, full)


def shift(value, axis, size, by):
    return lax.ppermute(value, axis, [(i, (i + by) % size) for i in range(size)])


def spread(sums, axes, size):
    wide = jnp.broadcast_to(sums[None], (size,) + sums.shape)
    return lax.all_to_all(wide, axes, 0, 0, tiled=True)


def body(x, q, k, v, g, w, m, s):
    x_turned = turn(x[0])
    packed = pack(q[0], k[0], v[0], g[0])
    heads = lax.all_to_all(packed, ("y", "core"), 0, 0, tiled=True).reshape(LENGTH, PACKED)
    x_full = lax.all_gather(x_turned, ("y", "core"), axis=0, tiled=False)
    grouped = attention(heads)

    at_x = lax.axis_index("x")
    place_x = at_x.reshape(1).astype(jnp.int32)
    part_a = project_a(place_x, grouped, x_full)
    part_b = project_b(place_x, grouped, x_full)
    part_a = lax.psum_scatter(part_a, "z", scatter_dimension=0, tiled=True)[0]
    part_b = fold([part_b[0]] + [shift(part_b[by], "x", NX, by) for by in range(1, NX)])
    part_b = lax.all_to_all(part_b, "z", 0, 0, tiled=True)
    part_a = [part_a[0]] + [shift(part_a[by], "x", NX, by) for by in range(1, NX)]

    first_new, second_new, direction, mine_a, mine_b, sums = optimizer(part_a, part_b, w, m, s)
    place = jnp.stack([at_x, (at_x + 3) % NX, (at_x + 1) % NX, (at_x + 2) % NX]).astype(jnp.int32)
    pieces = (
        mine_a,
        shift(mine_a, "x", NX, 1),
        shift(mine_a, "x", NX, -1),
        shift(mine_a, "x", NX, 2),
    )
    gathered_b = lax.all_gather(mine_b, "z", axis=0, tiled=False)
    sums = spread(jnp.sum(spread(sums, ("y", "core"), 8), axis=0), ("x", "z"), 32)
    new_a = apply_step(apply_a_kernel, (place, sums, *pieces), NX, ROWS_A, "apply_a")
    new_b = apply_step(apply_b_kernel, (sums, gathered_b), NZ, ROWS_B, "apply_b")
    full_a = lax.all_gather(new_a, "z", axis=0, tiled=False)
    before, after = shift(new_b, "x", NX, 1), shift(new_b, "x", NX, -1)
    far_lo = shift(before[: NZ // 2], "x", NX, 1)
    far_hi = shift(after[NZ // 2 :], "x", NX, -1)
    new_weights = join_x(place, new_b, before, after, far_lo, far_hi)
    new_weights = join_sc(new_weights, full_a)

    total = jnp.sum(sums, axis=0)
    lamb_update = (jnp.sqrt(total[0, 0]) / jnp.sqrt(total[1, 0])) * direction
    return first_new, second_new, lamb_update, new_weights.reshape(WIDTH, COLS)


def solution(mesh):
    fine = Mesh(mesh.devices.reshape(NX, NZ, NY, NCORE), ("x", "z", "y", "core"))
    dp, ctx = ("x", "z"), ("y", "core")
    seq = P(dp, ctx, None)
    mat = P(dp, ctx)
    return jax.shard_map(
        body,
        mesh=fine,
        in_specs=(seq, seq, seq, seq, seq, mat, mat, mat),
        out_specs=(mat, mat, mat, P(None, ctx)),
        check_vma=False,
    )
```
